512 devices in a mesh: ctx: 64 (over y, z), head: 8 (over x, core).
Axes of the slice: x: 4, y: 4, z: 16, core: 2. Of those that a mesh axis runs over, the one named last changes fastest.
Arguments:
- queries: bfloat16 [4096, 32, 128], P(('ctx', 'head')), may hold values from -12 to 12
- fresh_keys: bfloat16 [4096, 8, 128], P(('ctx', 'head')), may hold values from -12 to 12
- fresh_values: bfloat16 [4096, 8, 128], P(('ctx', 'head')), may hold values from -6 to 6
- cache_keys: bfloat16 [262144, 8, 128], P('ctx', 'head'), may hold values from -12 to 12
- cache_values: bfloat16 [262144, 8, 128], P('ctx', 'head'), may hold values from -6 to 6
- selected: int32 [32, 12], replicated, may hold values from 0 to 63, all different within a row; in each aligned block of 32 rows (0 to 31, 32 to 63, ...) at most 6 rows name the same one
- start: int32 [1], replicated, may hold values from 253953 to 262144
Outputs:
- attended: bfloat16 [4096, 32, 128], P(('ctx', 'head'))
The draws below stay inside these ranges and needn't reach their ends.
Inputs may be any that keep to these rules, and one draw needn't show every extreme that they name: Row t lists 12 different blocks selected by query tile t; no block is listed by more than 6 tiles, and some block by exactly 6.
All inputs are finite; a program needn't handle non-finite values.
Results may differ from the reference program's by a relative error of at most 0.0033.
Values may be sent and summed in bfloat16 or wider, within the bound.
No kernel may reach another device: no remote copies, remote signals or barrier semaphores. Data moves between devices by JAX's collectives and lax.ppermute only.
A program may use at most 128 MiB of HBM per device.

```python
import math
import jax
import jax.numpy as jnp
import numpy as np
from jax import lax

HD = 128
QH = 32
KVH = 8
TILE = 128
SEL = 12
BLK = 4096
NTOK = 4096
TILES = 32
NBLK = 64
CAP = 6


def draw_queries(key, part):
    base = jax.random.normal(jax.random.fold_in(key, 1), (NTOK, QH, HD), jnp.float32)
    base = base * 3.0
    return jnp.clip(base, -12.0, 12.0).astype(jnp.bfloat16)


def draw_fresh_keys(key, part):
    base = jax.random.normal(jax.random.fold_in(key, 2), (NTOK, KVH, HD), jnp.float32)
    return jnp.clip(base, -12.0, 12.0).astype(jnp.bfloat16)


def draw_cache_keys(key, part):
    base = jax.random.normal(jax.random.fold_in(key, 4), (NBLK * BLK, KVH, HD), jnp.float32)
    return jnp.clip(base, -6.0, 6.0).astype(jnp.bfloat16)


def level_of(stream_key, dims, split, least, largest):
    def one(axis_at, blocks):
        heights = jax.random.uniform(jax.random.fold_in(jax.random.fold_in(stream_key, 6), axis_at), (blocks,), jnp.float32, least / len(split), largest / len(split))
        return jnp.repeat(jnp.exp(heights), dims[axis_at] // blocks).reshape((-1,) + (1,) * (len(dims) - axis_at - 1))

    loudness = one(*split[0])
    for cut in split[1:]:
        loudness = loudness * one(*cut)
    return loudness


def assign_block(stream_key, own, number, rows, amount, top, most, slope):
    sequence = jax.random.permutation(stream_key, amount)
    packed, ordinary = portions_of(amount, rows * top, most, slope, True), portions_of(amount, rows * top, most, slope, False)
    places = jnp.arange(amount)

    def named(sizes, rotation):
        used = int((sizes > 0).sum())
        fixed = max(1, used // 4)
        shifted = fixed + (places - fixed + rotation * (used - fixed)) % max(1, amount - fixed)
        return jnp.zeros((amount,), jnp.int32).at[sequence[jnp.where(places < fixed, places, shifted)]].set(jnp.asarray(sizes, jnp.int32))

    sizes = jnp.where(number % 4 == 0, named(packed, number // 4), named(ordinary, number - number // 4 - 1))
    mixed = jax.random.permutation(jax.random.fold_in(own, 3), amount)
    giver, sink = mixed[0:amount // 2 * 2:2], mixed[1:amount // 2 * 2:2]
    margin = jnp.minimum(sizes[giver] - 1, most - sizes[sink]) // 2
    margin = jnp.where((giver == sequence[0]) | (sink == sequence[0]) | (sizes[sink] == 0), 0, jnp.maximum(margin, 0))
    shifted = jax.random.randint(jax.random.fold_in(own, 4), (amount // 2,), 0, 1 << 20) % (margin + 1)
    sizes = sizes.at[giver].add(-shifted).at[sink].add(shifted)
    labels = jnp.searchsorted(jnp.cumsum(sizes), jnp.arange(rows * top), side="right").astype(jnp.int32)
    listing = labels.reshape(top, rows).T
    listing = listing[jax.random.permutation(jax.random.fold_in(own, 1), rows)]
    rotation = jax.random.randint(jax.random.fold_in(own, 2), (rows, 1), 0, top)
    return jnp.take_along_axis(listing, (jnp.arange(top)[None, :] + rotation) % top, axis=1)


def portions_of(amount, total, bound, skew, full):
    portions = [(1 << 20) // math.isqrt(grade ** skew) + 1 for grade in range(1, amount + 1)]
    largest = bound if full else min(bound, max(-(-total // amount), total * portions[0] // sum(portions)))
    least = 1 if total - largest >= amount - 1 else 0
    given, rest = [largest] + [least] * (amount - 1), total - largest - least * (amount - 1)
    while rest > 0:
        candidates = [i for i in range(1, amount) if given[i] < largest] or [i for i in range(1, amount) if given[i] < bound]
        whole, left = sum([portions[i] for i in candidates]), rest
        for i in candidates:
            extra = min(bound - given[i], max(1, left * portions[i] // whole), rest)
            given[i] = given[i] + extra
            rest = rest - extra
    return np.array(given)


def scatter_about(own_key, extent, scale, bound, cuts=(), kind=jnp.bfloat16):
    level = level_of(own_key, extent, cuts, -0.22, 0.18) if cuts else 1.0
    entries = jax.random.normal(own_key, extent, jnp.float32) * scale * level
    return jnp.minimum(jnp.maximum(entries, -bound), bound).astype(kind)


def setup_inputs(seed: int = 0) -> dict:
    streams_of = jax.random.split(jax.random.key(seed), 8)
    queries = draw_queries(jax.random.fold_in(streams_of[7], 71), 0)
    fresh_keys = draw_fresh_keys(jax.random.fold_in(streams_of[7], 71), 0)
    fresh_values = scatter_about(streams_of[2], (NTOK, KVH, HD), 1.0, 6.0, ((0, 512),))
    cache_keys = draw_cache_keys(jax.random.fold_in(streams_of[7], 71), 0)
    cache_values = scatter_about(streams_of[4], (NBLK * BLK, KVH, HD), 1.0, 6.0, ((0, 64), (1, 8)))
    selected_keys = jax.random.split(jax.random.fold_in(streams_of[5], 1), TILES // TILES)
    selected_turns = jax.random.permutation(jax.random.fold_in(streams_of[5], 3), TILES // TILES)
    selected = jax.vmap(lambda own, number: assign_block(jax.random.fold_in(streams_of[5], 2), own, number, TILES, NBLK, SEL, CAP, 2))(selected_keys, selected_turns).reshape((TILES, SEL))
    start = jax.random.randint(streams_of[6], (1,), (NBLK - 2) * BLK + 1, NBLK * BLK + 1).astype(jnp.int32)
    return {"queries": queries, "fresh_keys": fresh_keys, "fresh_values": fresh_values, "cache_keys": cache_keys, "cache_values": cache_values, "selected": selected, "start": start}


masked_score = -1.0e30


def part_terms(query_tile, key_block, value_block, allowed):
    tile_rows = query_tile.shape[0]
    per_group = QH // KVH
    grouped = query_tile.astype(jnp.float32).reshape(tile_rows, KVH, per_group, HD)
    scores = jnp.einsum("tkgd,nkd->kgtn", grouped, key_block.astype(jnp.float32)) * (HD ** -0.5)
    scores = jnp.where(allowed[None, None], scores, masked_score)
    maxima = jnp.max(scores, axis=-1)
    weights = jnp.where(allowed[None, None], jnp.exp(scores - maxima[..., None]), 0.0)
    totals = jnp.sum(weights, axis=-1)
    rounded = lax.optimization_barrier(weights.astype(jnp.bfloat16))
    sums = jnp.einsum("kgtn,nkd->kgtd", rounded.astype(jnp.float32), value_block.astype(jnp.float32))
    return maxima, totals, sums


def join_parts(first_part, second_part):
    joined_max = jnp.maximum(first_part[0], second_part[0])
    first_scale = jnp.exp(first_part[0] - joined_max)
    second_scale = jnp.exp(second_part[0] - joined_max)
    totals = first_part[1] * first_scale + second_part[1] * second_scale
    sums = first_part[2] * first_scale[..., None] + second_part[2] * second_scale[..., None]
    return joined_max, totals, sums


def reference(queries, fresh_keys, fresh_values, cache_keys, cache_values, selected, start):
    limit = start[0]

    def one_tile(tile_index):
        query_tile = lax.dynamic_slice_in_dim(queries, tile_index * TILE, TILE, 0)
        query_pos = tile_index * TILE + jnp.arange(TILE, dtype=jnp.int32)
        key_pos = jnp.arange(NTOK, dtype=jnp.int32)
        state = part_terms(query_tile, fresh_keys, fresh_values, key_pos[None, :] <= query_pos[:, None])

        def add_block(running, block_id):
            key_block = lax.dynamic_slice_in_dim(cache_keys, block_id * BLK, BLK, 0)
            value_block = lax.dynamic_slice_in_dim(cache_values, block_id * BLK, BLK, 0)
            cache_pos = block_id * BLK + jnp.arange(BLK, dtype=jnp.int32)
            allowed = jnp.broadcast_to((cache_pos < limit)[None, :], (TILE, BLK))
            terms = part_terms(query_tile, key_block, value_block, allowed)
            return join_parts(running, terms), None

        state, _ = lax.scan(add_block, state, selected[tile_index])
        result = state[2] / state[1][..., None]
        return jnp.transpose(result, (2, 0, 1, 3)).reshape(TILE, QH, HD).astype(jnp.bfloat16)

    tiles_out = lax.map(one_tile, jnp.arange(TILES, dtype=jnp.int32))
    return tiles_out.reshape(NTOK, QH, HD)
```

```python
import functools
import math

import jax
import jax.numpy as jnp
from jax import lax
from jax.experimental import pallas as pl
from jax.experimental.pallas import tpu as pltpu
from jax.sharding import PartitionSpec as P

TILE = 128
CHUNKS = 2
KEYS = 512
NEG = -1e30


def plan_kernel(tiles, sel, capacity, me_ref, sel_ref, tile_ref, index_ref, own_ref, count_ref):
    me, per_tile = me_ref[0], me_ref[1]

    def clear(b, _):
        count_ref[b] = 0
        return 0

    lax.fori_loop(0, count_ref.shape[0], clear, 0)
    for i in range(capacity):
        tile_ref[i] = 0

    own_tile = me // per_tile

    def one_tile(t, _):
        hit = jnp.int32(-1)
        for k in range(sel):
            b = sel_ref[t, k]
            slot = jnp.minimum(count_ref[b], capacity - 1)
            count_ref[b] = count_ref[b] + 1
            hit = jnp.where(b == me, slot, hit)
            own_ref[k] = jnp.where(t == own_tile, b * capacity + slot, own_ref[k])
            index_ref[tiles * sel + k] = b * capacity + slot

        @pl.when(hit >= 0)
        def _():
            tile_ref[hit] = t
            for k in range(sel):
                index_ref[hit * sel + k] = index_ref[tiles * sel + k]

        return 0

    for k in range(sel):
        own_ref[k] = 0
    lax.fori_loop(0, tiles, one_tile, 0)


def plan(selected, ctx_index, per_tile, capacity, blocks):
    tiles, sel = selected.shape
    smem = pl.BlockSpec(memory_space=pltpu.SMEM)
    tile_ids, index, own = pl.pallas_call(
        functools.partial(plan_kernel, tiles, sel, capacity),
        out_shape=(
            jax.ShapeDtypeStruct((capacity,), jnp.int32),
            jax.ShapeDtypeStruct(((tiles + 1) * sel,), jnp.int32),
            jax.ShapeDtypeStruct((sel,), jnp.int32),
        ),
        in_specs=[smem, smem],
        out_specs=(smem, smem, smem),
        scratch_shapes=[pltpu.SMEM((blocks,), jnp.int32)],
        name="plan",
    )(jnp.stack([ctx_index, jnp.int32(per_tile)]), selected)
    return tile_ids, index, own


def column_to_row(column):
    return jnp.broadcast_to(column, (column.shape[0], 128)).T[0:1, :]


def row_to_columns(row):
    return jnp.broadcast_to(row, (128, row.shape[1])).T


def keep(block, width, limit):
    return block * width + lax.broadcasted_iota(jnp.int32, (1, width), 1) < limit


def max_kernel(tile_ref, valid_ref, q_ref, kt_ref, wide_ref, row_ref):
    q = q_ref[0]
    rows = q.shape[0]
    length = kt_ref.shape[1]
    valid = valid_ref[0]

    def run(masked):
        best = None
        for j in range(length // KEYS):
            s = jnp.dot(q, kt_ref[:, j * KEYS : (j + 1) * KEYS], preferred_element_type=jnp.float32)
            if masked:
                s = jnp.where(keep(j, KEYS, valid), s, NEG)
            for g in range(KEYS // 128):
                part = s[:, g * 128 : (g + 1) * 128]
                best = part if best is None else jnp.maximum(best, part)
        top = jnp.max(best, axis=1, keepdims=True)
        wide_ref[0] = jnp.broadcast_to(top, (rows, 128))
        row_ref[0] = column_to_row(top)

    pl.when(valid == length)(lambda: run(False))
    pl.when(valid != length)(lambda: run(True))


def block_max(tile_ids, valid, q, kt):
    capacity = tile_ids.shape[0]
    rows = q.shape[1]
    return pl.pallas_call(
        max_kernel,
        out_shape=(
            jax.ShapeDtypeStruct((capacity, rows, 128), jnp.float32),
            jax.ShapeDtypeStruct((capacity, 1, rows), jnp.float32),
        ),
        grid_spec=pltpu.PrefetchScalarGridSpec(
            num_scalar_prefetch=2,
            grid=(capacity,),
            in_specs=[
                pl.BlockSpec((1, rows, 128), lambda i, t, v: (t[i], 0, 0)),
                pl.BlockSpec(kt.shape, lambda i, t, v: (0, 0)),
            ],
            out_specs=(
                pl.BlockSpec((1, rows, 128), lambda i, t, v: (i, 0, 0)),
                pl.BlockSpec((1, 1, rows), lambda i, t, v: (i, 0, 0)),
            ),
        ),
        name="block_max",
    )(tile_ids, valid, q, kt)


def gathered_max(stats_ref, index_ref, first, sel):
    best = stats_ref[pl.ds(index_ref[first], 1), :]
    for k in range(1, sel):
        best = jnp.maximum(best, stats_ref[pl.ds(index_ref[first + k], 1), :])
    return best


def sum_kernel(
    factor, sel, tile_ref, valid_ref, index_ref, q_ref, kt_ref, v_ref, wide_ref, stats_ref, zero_ref, out_ref
):
    del zero_ref
    i = pl.program_id(0)
    q = q_ref[0]
    rows = q.shape[0]
    length = kt_ref.shape[1]
    valid = valid_ref[0]
    half = rows // 2
    row_top = gathered_max(stats_ref, index_ref, i * sel, sel)

    def run(masked):
        top = wide_ref[0]
        tops = jnp.concatenate([top] * (KEYS // 128), axis=1)
        total = jnp.zeros((rows, 128), jnp.float32)
        acc = jnp.zeros((rows, 128), jnp.float32)
        for j in range(length // KEYS):
            s = jnp.dot(q, kt_ref[:, j * KEYS : (j + 1) * KEYS], preferred_element_type=jnp.float32)
            p = jnp.exp2((s - tops) * factor)
            if masked:
                p = jnp.where(keep(j, KEYS, valid), p, 0.0)
            for g in range(KEYS // 128):
                total += p[:, g * 128 : (g + 1) * 128]
            acc += jnp.dot(
                p.astype(jnp.bfloat16),
                v_ref[j * KEYS : (j + 1) * KEYS, :],
                preferred_element_type=jnp.float32,
            )
        shrink = jnp.exp2((top - row_to_columns(row_top)) * factor)
        acc = acc * shrink
        sums = column_to_row(jnp.sum(total, axis=1, keepdims=True) * shrink[:, 0:1])
        for side in range(2):
            out_ref[0, side, 0:half, :] = acc[side * half : (side + 1) * half]
            out_ref[0, side, half : half + 8, :] = jnp.broadcast_to(
                sums[:, side * half : (side + 1) * half], (8, half)
            )

    pl.when(valid == length)(lambda: run(False))
    pl.when(valid != length)(lambda: run(True))


def block_sum(factor, tile_ids, valid, index, q, kt, v, wide, stats, zeros):
    capacity = tile_ids.shape[0]
    rows = q.shape[1]
    sel = index.shape[0] // (q.shape[0] + 1)
    return pl.pallas_call(
        functools.partial(sum_kernel, factor, sel),
        out_shape=jax.ShapeDtypeStruct(zeros.shape, jnp.float32),
        grid_spec=pltpu.PrefetchScalarGridSpec(
            num_scalar_prefetch=3,
            grid=(capacity,),
            in_specs=[
                pl.BlockSpec((1, rows, 128), lambda i, t, v, x: (t[i], 0, 0)),
                pl.BlockSpec(kt.shape, lambda i, t, v, x: (0, 0)),
                pl.BlockSpec(v.shape, lambda i, t, v, x: (0, 0)),
                pl.BlockSpec((1, rows, 128), lambda i, t, v, x: (i, 0, 0)),
                pl.BlockSpec(stats.shape, lambda i, t, v, x: (0, 0)),
                pl.BlockSpec(memory_space=pl.ANY),
            ],
            out_specs=pl.BlockSpec((1,) + zeros.shape[1:], lambda i, t, v, x: (t[i], 0, 0, 0)),
        ),
        input_output_aliases={8: 0},
        name="block_sum",
    )(tile_ids, valid, index, q, kt, v, wide, stats, zeros)


def fresh_kernel(factor, tokens, me_ref, q_ref, k_ref, v_ref, acc_ref, top_ref, total_ref, s_ref):
    rows = q_ref.shape[0]
    first = me_ref[0] * tokens
    steps = (first + tokens + KEYS - 1) // KEYS
    position = first + lax.rem(lax.broadcasted_iota(jnp.int32, (rows, KEYS), 0), tokens)
    column = lax.broadcasted_iota(jnp.int32, (rows, KEYS), 1)
    top_ref[...] = jnp.full((rows, 128), NEG, jnp.float32)

    def score(j, _):
        key = k_ref[pl.ds(pl.multiple_of(j * KEYS, KEYS), KEYS), :]
        s = lax.dot_general(
            q_ref[...], key, (((1,), (1,)), ((), ())), preferred_element_type=jnp.float32
        )
        s = jnp.where(column + j * KEYS <= position, s, NEG)
        s_ref[j] = s
        best = top_ref[...]
        for g in range(KEYS // 128):
            best = jnp.maximum(best, s[:, g * 128 : (g + 1) * 128])
        top_ref[...] = best
        return 0

    lax.fori_loop(0, steps, score, 0)
    top_ref[...] = jnp.broadcast_to(jnp.max(top_ref[...], axis=1, keepdims=True), (rows, 128))
    acc_ref[...] = jnp.zeros((rows, 128), jnp.float32)
    total_ref[...] = jnp.zeros((rows, 128), jnp.float32)

    def weigh(j, _):
        tops = jnp.concatenate([top_ref[...]] * (KEYS // 128), axis=1)
        p = jnp.exp2((s_ref[j] - tops) * factor)
        total = total_ref[...]
        for g in range(KEYS // 128):
            total += p[:, g * 128 : (g + 1) * 128]
        total_ref[...] = total
        acc_ref[...] += jnp.dot(
            p.astype(jnp.bfloat16),
            v_ref[pl.ds(pl.multiple_of(j * KEYS, KEYS), KEYS), :],
            preferred_element_type=jnp.float32,
        )
        return 0

    lax.fori_loop(0, steps, weigh, 0)
    total_ref[...] = jnp.broadcast_to(jnp.sum(total_ref[...], axis=1, keepdims=True), (rows, 128))


def fresh_part(factor, tokens, me, q, k, v):
    rows = q.shape[0]
    wide = jax.ShapeDtypeStruct((rows, 128), jnp.float32)
    vmem = pl.BlockSpec(memory_space=pltpu.VMEM)
    return pl.pallas_call(
        functools.partial(fresh_kernel, factor, tokens),
        out_shape=(wide, wide, wide),
        in_specs=[pl.BlockSpec(memory_space=pltpu.SMEM), vmem, vmem, vmem],
        out_specs=(vmem, vmem, vmem),
        scratch_shapes=[pltpu.VMEM((k.shape[0] // KEYS, rows, KEYS), jnp.float32)],
        name="fresh_part",
    )(me, q, k, v)


def join_kernel(factor, sel, own_ref, side_ref, acc_ref, top_ref, total_ref, *refs):
    out_ref = refs[-1]
    chunks = (len(refs) - 1) // 2
    side = side_ref[0]
    for c in range(chunks):
        stats_ref, back_ref = refs[2 * c], refs[2 * c + 1]
        half = back_ref.shape[0] - 8
        row = gathered_max(stats_ref, own_ref, 0, sel)
        row = jnp.where(side == 0, row[:, 0:half], row[:, half : 2 * half])
        cache_top = row_to_columns(row)
        here = slice(c * half, (c + 1) * half)
        top = jnp.maximum(cache_top, top_ref[here, :])
        cache_scale = jnp.exp2((cache_top - top) * factor)
        own_scale = jnp.exp2((top_ref[here, :] - top) * factor)
        cache_total = row_to_columns(back_ref[half : half + 1, :])
        upper = acc_ref[here, :] * own_scale + back_ref[0:half, :] * cache_scale
        lower = total_ref[here, :] * own_scale + cache_total * cache_scale
        out_ref[here, :] = (upper / lower).astype(jnp.bfloat16)


def join(factor, own, side, acc, top, total, stats, back):
    vmem = pl.BlockSpec(memory_space=pltpu.VMEM)
    smem = pl.BlockSpec(memory_space=pltpu.SMEM)
    pairs = [x for pair in zip(stats, back) for x in pair]
    return pl.pallas_call(
        functools.partial(join_kernel, factor, own.shape[0]),
        out_shape=jax.ShapeDtypeStruct(acc.shape, jnp.bfloat16),
        in_specs=[smem, smem] + [vmem] * (3 + len(pairs)),
        out_specs=vmem,
        name="join",
    )(own, side, acc, top, total, *pairs)


def shards(queries, fresh_keys, fresh_values, cache_keys, cache_values, selected, start):
    part, q_heads, head_size = queries.shape
    kv_heads = fresh_keys.shape[1]
    group = q_heads // kv_heads
    heads_axis = lax.axis_size("head")
    ctx_size = lax.axis_size("ctx")
    ctx_index = lax.axis_index("ctx")
    tokens = part * heads_axis
    per_tile = TILE // tokens
    tiles, sel = selected.shape
    blocks = ctx_size
    capacity = tiles * sel // blocks
    factor = head_size**-0.5 * math.log2(math.e)
    length = cache_keys.shape[0]

    mixed = jnp.concatenate(
        [
            queries.reshape(part, kv_heads, group, head_size),
            fresh_keys[:, :, None],
            fresh_values[:, :, None],
        ],
        axis=2,
    ).transpose(1, 2, 0, 3)
    mixed = lax.all_to_all(mixed, "head", split_axis=0, concat_axis=0, tiled=True)
    mixed = mixed.transpose(1, 0, 2, 3).reshape(group + 2, tokens, head_size)
    own_q = mixed[:group].reshape(group * tokens, head_size)

    rows = group * tokens // CHUNKS
    gathered = [
        lax.all_gather(own_q[c * rows : (c + 1) * rows], "ctx", axis=0, tiled=True).reshape(
            tiles, per_tile * rows, head_size
        )
        for c in range(CHUNKS)
    ]
    fresh = lax.all_gather(mixed[group:], "ctx", axis=1, tiled=False)
    fresh = fresh.reshape(2, ctx_size * tokens, head_size)

    kt = cache_keys[:, 0].T
    v = cache_values[:, 0]
    tile_ids, index, own = plan(selected, ctx_index, per_tile, capacity, blocks)
    valid = jnp.clip(start - ctx_index * length, 0, length)

    tops = [block_max(tile_ids, valid, q, kt) for q in gathered]
    stats = [
        lax.all_gather(row[:, 0], "ctx", axis=0, tiled=True) for _, row in tops
    ]
    back = []
    for c in range(CHUNKS):
        zeros = jnp.zeros((tiles, per_tile, rows + 8, head_size), jnp.float32)
        spread = block_sum(
            factor, tile_ids, valid, index, gathered[c], kt, v, tops[c][0], stats[c], zeros
        )
        spread = spread.reshape(ctx_size * (rows + 8), head_size)
        back.append(lax.psum_scatter(spread, "ctx", scatter_dimension=0, tiled=True))
    acc, top, total = fresh_part(factor, tokens, ctx_index.reshape(1), own_q, fresh[0], fresh[1])
    side = (ctx_index % per_tile).reshape(1)
    result = join(factor, own, side, acc, top, total, stats, back)
    result = result.reshape(group, heads_axis, part, head_size).transpose(1, 0, 2, 3)
    result = lax.all_to_all(result, "head", split_axis=0, concat_axis=0, tiled=True)
    return result.reshape(q_heads, part, head_size).transpose(1, 0, 2)


def solution(mesh):
    in_specs = (
        P(("ctx", "head"), None, None),
        P(("ctx", "head"), None, None),
        P(("ctx", "head"), None, None),
        P("ctx", "head", None),
        P("ctx", "head", None),
        P(),
        P(),
    )
    out_specs = P(("ctx", "head"), None, None)
    return jax.shard_map(shards, mesh=mesh, in_specs=in_specs, out_specs=out_specs, check_vma=False)
```

```python
import functools
import math

import jax
import jax.numpy as jnp
from jax import lax
from jax.experimental import pallas as pl
from jax.experimental.pallas import tpu as pltpu
from jax.sharding import PartitionSpec as P

TILE = 128
RING = 16
KEYS = 512
NEG = -1e30
NONE = -4000.0
FINE = 2.0**19
FULL = 32767.0


def plan_kernel(ring, per_row, me_ref, sel_ref, tile_ref, flag_ref):
    tiles, sel = sel_ref.shape
    me = me_ref[0]
    y, z = me // ring, lax.rem(me, ring)
    for i in range(tile_ref.shape[0]):
        tile_ref[i] = 0
    for i in range(flag_ref.shape[0]):
        flag_ref[i] = 0

    def one_tile(t, count):
        hit = jnp.int32(0)
        mine = t // per_row == y
        for k in range(sel):
            b = sel_ref[t, k]
            hit = jnp.where(b == me, 1, hit)

            @pl.when(mine & (lax.rem(b, ring) == z))
            def _():
                flag_ref[(b // ring) * per_row + lax.rem(t, per_row)] = 1

        @pl.when(hit == 1)
        def _():
            tile_ref[jnp.minimum(count, tile_ref.shape[0] - 1)] = t

        return count + hit

    lax.fori_loop(0, tiles, one_tile, jnp.int32(0))


def plan(selected, me, ring, per_row, capacity, rows_of_chips):
    smem = pl.BlockSpec(memory_space=pltpu.SMEM)
    return pl.pallas_call(
        functools.partial(plan_kernel, ring, per_row),
        out_shape=(
            jax.ShapeDtypeStruct((capacity,), jnp.int32),
            jax.ShapeDtypeStruct((rows_of_chips * per_row,), jnp.int32),
        ),
        in_specs=[smem, smem],
        out_specs=(smem, smem),
        name="plan",
    )(me, selected)


def row_to_columns(row):
    return jnp.broadcast_to(row, (128, row.shape[1])).T


def pack(out_view, acc, level):
    rows = acc.shape[0]
    largest = jnp.maximum(jnp.max(jnp.abs(acc), axis=1, keepdims=True), 1e-30)
    code = jnp.round(acc * (FULL / largest)).astype(jnp.int32)
    out_view[0:rows, :] = code.astype(jnp.int16)
    lane = lax.broadcasted_iota(jnp.int32, (rows, 128), 1)
    both = jnp.where(lane == 0, level, jnp.log2(largest)).T[0:8, :]
    whole = jnp.round(jnp.clip(both, NONE, -NONE) * FINE).astype(jnp.int32)
    high = whole >> 16
    low = (whole & 0xFFFF) - 32768
    rank = lax.broadcasted_iota(jnp.int32, (8, 128), 0)
    stats = jnp.zeros((8, 128), jnp.int32)
    n = rows // 128
    for k, source in enumerate((high, low)):
        for stat in range(2):
            for g in range(n):
                piece = jnp.broadcast_to(source[stat : stat + 1, g * 128 : (g + 1) * 128], (8, 128))
                stats = jnp.where(rank == (k * 2 + stat) * n + g, piece, stats)
    out_view[rows : rows + 8, :] = stats.astype(jnp.int16)


def unpack_stats(view, rows):
    n = rows // 128
    raw = view[rows : rows + 8, :].astype(jnp.int32)
    found = []
    for stat in range(2):
        high = [raw[stat * n + g : stat * n + g + 1, :] for g in range(n)]
        low = [raw[(2 + stat) * n + g : (2 + stat) * n + g + 1, :] for g in range(n)]
        whole = [(h << 16) + (w + 32768) for h, w in zip(high, low)]
        found.append(jnp.concatenate([w.astype(jnp.float32) for w in whole], axis=1) * (1.0 / FINE))
    return found


def block_kernel(
    factor, tile_ref, valid_ref, q_ref, next_ref, kt_ref, v_ref, out_ref, s0_ref, s1_ref, top_ref, total_ref, acc_ref
):
    i = pl.program_id(0)
    length = kt_ref.shape[1]
    rows = q_ref.shape[3]
    valid = valid_ref[0]
    steps = length // KEYS

    def score(q, s_ref, slot, j):
        s = jnp.dot(q, kt_ref[:, j * KEYS : (j + 1) * KEYS], preferred_element_type=jnp.float32)
        position = lax.broadcasted_iota(jnp.int32, (1, KEYS), 1) + j * KEYS
        s = s + jnp.where(position < valid, 0.0, NEG)
        s_ref[:, j * KEYS : (j + 1) * KEYS] = s
        best = s[:, 0:128]
        for g in range(1, KEYS // 128):
            best = jnp.maximum(best, s[:, g * 128 : (g + 1) * 128])
        if j:
            best = jnp.maximum(best, top_ref[slot])
        if j == steps - 1:
            best = jnp.broadcast_to(jnp.max(best, axis=1, keepdims=True), (rows, 128))
        top_ref[slot] = best

    def weigh(s_ref, slot, j):
        tops = jnp.concatenate([top_ref[slot]] * (KEYS // 128), axis=1)
        p = jnp.exp2((s_ref[:, j * KEYS : (j + 1) * KEYS] - tops) * factor)
        total = p[:, 0:128]
        for g in range(1, KEYS // 128):
            total += p[:, g * 128 : (g + 1) * 128]
        product = jnp.dot(
            p.astype(jnp.bfloat16), v_ref[j * KEYS : (j + 1) * KEYS, :], preferred_element_type=jnp.float32
        )
        total_ref[...] = total_ref[...] + total if j else total
        acc_ref[...] = acc_ref[...] + product if j else product

    def finish(slot):
        total = jnp.sum(total_ref[...], axis=1, keepdims=True)
        level = top_ref[slot][:, 0:1] * factor + jnp.log2(total)
        level = jnp.where(valid > 0, level, NONE)
        pack(out_ref.at[0, 0, slot], acc_ref[...] / total, level)

    @pl.when(i == 0)
    def _():
        for j in range(steps):
            score(q_ref[0, 0, 0], s0_ref, 0, j)

    for j in range(steps):
        score(q_ref[0, 1, 0], s1_ref, 1, j)
        weigh(s0_ref, 0, j)
    finish(0)
    for j in range(steps):
        score(next_ref[0, 0, 0], s0_ref, 0, j)
        weigh(s1_ref, 1, j)
    finish(1)


def block_part(factor, tile_ids, valid, q, kt, v):
    per_row, sides, tile_rows, rows, _ = q.shape
    capacity = tile_ids.shape[0]
    return pl.pallas_call(
        functools.partial(block_kernel, factor),
        out_shape=jax.ShapeDtypeStruct((tile_rows, per_row, sides, rows + 8, 128), jnp.int16),
        grid_spec=pltpu.PrefetchScalarGridSpec(
            num_scalar_prefetch=2,
            grid=(capacity,),
            in_specs=[
                pl.BlockSpec(
                    (1, sides, 1, rows, 128),
                    lambda i, t, n: (lax.rem(t[i], per_row), 0, t[i] // per_row, 0, 0),
                ),
                pl.BlockSpec(
                    (1, 1, 1, rows, 128),
                    lambda i, t, n: (
                        lax.rem(t[jnp.minimum(i + 1, capacity - 1)], per_row),
                        0,
                        t[jnp.minimum(i + 1, capacity - 1)] // per_row,
                        0,
                        0,
                    ),
                ),
                pl.BlockSpec(kt.shape, lambda i, t, n: (0, 0)),
                pl.BlockSpec(v.shape, lambda i, t, n: (0, 0)),
            ],
            out_specs=pl.BlockSpec(
                (1, 1, sides, rows + 8, 128), lambda i, t, n: (t[i] // per_row, lax.rem(t[i], per_row), 0, 0, 0)
            ),
            scratch_shapes=[
                pltpu.VMEM((rows, kt.shape[1]), jnp.float32),
                pltpu.VMEM((rows, kt.shape[1]), jnp.float32),
                pltpu.VMEM((2, rows, 128), jnp.float32),
                pltpu.VMEM((rows, 128), jnp.float32),
                pltpu.VMEM((rows, 128), jnp.float32),
            ],
        ),
        name="block_part",
    )(tile_ids, valid, q, q, kt, v)


def column_kernel(factor, ring, tokens, flag_ref, me_ref, q_ref, k_ref, v_ref, got_ref, out_ref, acc_ref, top_ref, total_ref):
    k, side = pl.program_id(0), pl.program_id(1)
    per_row = pl.num_programs(0)
    y, z = me_ref[0], me_ref[1]
    rows = q_ref.shape[3]
    sources = got_ref.shape[0]
    keys = k_ref.shape[0]
    q = q_ref[0, 0, 0]
    s = lax.dot_general(q, k_ref[...], (((1,), (1,)), ((), ())), preferred_element_type=jnp.float32)
    row = lax.broadcasted_iota(jnp.int32, (rows, keys), 0)
    column = lax.broadcasted_iota(jnp.int32, (rows, keys), 1)
    here = (y * ring + k * (ring // per_row) + side) * tokens + lax.rem(row, tokens)
    there = (column // tokens * ring + z) * tokens + lax.rem(column, tokens)
    allowed = there <= here
    top = jnp.max(jnp.where(allowed, s, NEG), axis=1, keepdims=True)
    p = jnp.where(allowed, jnp.exp2((s - top) * factor), 0.0)
    high = p.astype(jnp.bfloat16)
    low = (p - high.astype(jnp.float32)).astype(jnp.bfloat16)
    acc_ref[...] = jnp.dot(high, v_ref[...], preferred_element_type=jnp.float32) + jnp.dot(
        low, v_ref[...], preferred_element_type=jnp.float32
    )
    total_ref[...] = jnp.broadcast_to(jnp.sum(p, axis=1, keepdims=True), (rows, 128))
    top_ref[...] = jnp.broadcast_to(jnp.maximum(top * factor, NONE), (rows, 128))
    for sy in range(sources):

        @pl.when(flag_ref[sy * per_row + k] == 1)
        def _():
            level, largest = unpack_stats(got_ref.at[sy, 0, 0], rows)
            level = row_to_columns(level)
            size = row_to_columns(jnp.exp2(largest) * (1.0 / FULL))
            old = top_ref[...]
            new = jnp.maximum(old, level)
            shrink = jnp.exp2(old - new)
            weight = jnp.exp2(level - new)
            value = got_ref[sy, 0, 0, 0:rows, :].astype(jnp.int32).astype(jnp.float32)
            acc_ref[...] = acc_ref[...] * shrink + value * (weight * size)
            total_ref[...] = total_ref[...] * shrink + weight
            top_ref[...] = new

    total = jnp.maximum(total_ref[...], 1e-30)
    level = jnp.maximum(top_ref[...] + jnp.log2(total), NONE)[:, 0:1]
    pack(out_ref.at[0], acc_ref[...] / total, level)


def column_part(factor, ring, tokens, flags, me, q, k, v, got):
    per_row, sides, tile_rows, rows, _ = q.shape
    sources = got.shape[0]
    return pl.pallas_call(
        functools.partial(column_kernel, factor, ring, tokens),
        out_shape=jax.ShapeDtypeStruct((per_row * sides, rows + 8, 128), jnp.int16),
        grid_spec=pltpu.PrefetchScalarGridSpec(
            num_scalar_prefetch=2,
            grid=(per_row, sides),
            in_specs=[
                pl.BlockSpec((1, 1, 1, rows, 128), lambda i, h, f, m: (i, h, m[0], 0, 0)),
                pl.BlockSpec(k.shape, lambda i, h, f, m: (0, 0)),
                pl.BlockSpec(v.shape, lambda i, h, f, m: (0, 0)),
                pl.BlockSpec((sources, 1, 1, rows + 8, 128), lambda i, h, f, m: (0, i, h, 0, 0)),
            ],
            out_specs=pl.BlockSpec((1, rows + 8, 128), lambda i, h, f, m: (i * sides + h, 0, 0)),
            scratch_shapes=[pltpu.VMEM((rows, 128), jnp.float32)] * 3,
        ),
        name="column_part",
    )(flags, me, q, k, v, got)


def ring_kernel(got_ref, out_ref):
    sources, padded, _ = got_ref.shape
    rows = padded - 8
    stats = [unpack_stats(got_ref.at[s], rows) for s in range(sources)]
    top = functools.reduce(jnp.maximum, [level for level, _ in stats])
    weights = [jnp.exp2(level - top) for level, _ in stats]
    total = functools.reduce(jnp.add, weights)
    acc = jnp.zeros((rows, 128), jnp.float32)
    for s in range(sources):
        share = row_to_columns(weights[s] * jnp.exp2(stats[s][1]) / (FULL * total))
        acc += got_ref[s, 0:rows, :].astype(jnp.int32).astype(jnp.float32) * share
    out_ref[...] = acc.astype(jnp.bfloat16)


def ring_part(got):
    vmem = pl.BlockSpec(memory_space=pltpu.VMEM)
    return pl.pallas_call(
        ring_kernel,
        out_shape=jax.ShapeDtypeStruct((got.shape[1] - 8, 128), jnp.bfloat16),
        in_specs=[vmem],
        out_specs=vmem,
        name="ring_part",
    )(got)


def shards(queries, fresh_keys, fresh_values, cache_keys, cache_values, selected, start):
    part, q_heads, head_size = queries.shape
    kv_heads = fresh_keys.shape[1]
    group = q_heads // kv_heads
    heads_axis = lax.axis_size("head")
    ctx_size = lax.axis_size("ctx")
    ctx_index = lax.axis_index("ctx")
    ring = RING
    columns = ctx_size // ring
    across = [[y * ring + z for y in range(columns)] for z in range(ring)]
    along = [[y * ring + z for z in range(ring)] for y in range(columns)]
    tokens = part * heads_axis
    sides = TILE // tokens
    per_row = ring // sides
    tiles, sel = selected.shape
    capacity = tiles * sel // ctx_size
    factor = head_size**-0.5 * math.log2(math.e)
    length = cache_keys.shape[0]
    rows = group * tokens

    mixed = jnp.concatenate(
        [
            queries.reshape(part, kv_heads, group, head_size),
            fresh_keys[:, :, None],
            fresh_values[:, :, None],
        ],
        axis=2,
    ).transpose(1, 2, 0, 3)
    mixed = lax.all_to_all(mixed, "head", split_axis=0, concat_axis=0, tiled=True)
    mixed = mixed.transpose(1, 0, 2, 3).reshape(group + 2, tokens, head_size)

    column = jnp.broadcast_to(mixed[None], (columns,) + mixed.shape)
    column = lax.all_to_all(
        column, "ctx", split_axis=0, concat_axis=0, tiled=True, axis_index_groups=across
    )
    column_q = column[:, :group].reshape(columns, rows, head_size)
    column_k = column[:, group].reshape(columns * tokens, head_size)
    column_v = column[:, group + 1].reshape(columns * tokens, head_size)
    q = lax.all_gather(column_q, "ctx", axis=0, tiled=True, axis_index_groups=along)
    q = q.reshape(per_row, sides, columns, rows, head_size)

    kt = cache_keys[:, 0].T
    v = cache_values[:, 0]
    tile_ids, flags = plan(selected, ctx_index.reshape(1), ring, per_row, capacity, columns)
    valid = jnp.clip(start - ctx_index * length, 0, length)

    sent = block_part(factor, tile_ids, valid, q, kt, v)
    got = lax.all_to_all(
        sent, "ctx", split_axis=0, concat_axis=0, tiled=True, axis_index_groups=across
    )
    me = jnp.stack([ctx_index // ring, ctx_index % ring])
    sent = column_part(factor, ring, tokens, flags, me, q, column_k, column_v, got)
    got = lax.all_to_all(
        sent, "ctx", split_axis=0, concat_axis=0, tiled=True, axis_index_groups=along
    )
    result = ring_part(got)
    result = result.reshape(group, heads_axis, part, head_size).transpose(1, 0, 2, 3)
    result = lax.all_to_all(result, "head", split_axis=0, concat_axis=0, tiled=True)
    return result.reshape(q_heads, part, head_size).transpose(1, 0, 2)


def solution(mesh):
    in_specs = (
        P(("ctx", "head"), None, None),
        P(("ctx", "head"), None, None),
        P(("ctx", "head"), None, None),
        P("ctx", "head", None),
        P("ctx", "head", None),
        P(),
        P(),
    )
    out_specs = P(("ctx", "head"), None, None)
    return jax.shard_map(shards, mesh=mesh, in_specs=in_specs, out_specs=out_specs, check_vma=False)
```

```python
import functools
import math

import jax
import jax.numpy as jnp
from jax import lax
from jax.experimental import pallas as pl
from jax.experimental.pallas import tpu as pltpu
from jax.sharding import PartitionSpec as P

TILE = 128
RING = 16
KEYS = 512
CHUNKS = 2

NEG = -1e30
NONE = -4000.0
FINE = 2.0**19
FULL = 32767.0


def plan_kernel(ring, per_row, me_ref, sel_ref, tile_ref, flag_ref):
    tiles, sel = sel_ref.shape
    me = me_ref[0]
    y, z = me // ring, lax.rem(me, ring)
    rows = flag_ref.shape[0] // per_row
    for i in range(tile_ref.shape[0]):
        tile_ref[i] = 0
    for i in range(flag_ref.shape[0]):
        flag_ref[i] = 0

    def one_tile(t, count):
        hit = jnp.int32(0)
        mine = t // per_row == y
        for k in range(sel):
            b = sel_ref[t, k]
            hit = jnp.where(b == me, 1, hit)

            @pl.when(mine & (lax.rem(b, ring) == z))
            def _():
                flag_ref[lax.rem(y - b // ring + rows, rows) * per_row + lax.rem(t, per_row)] = 1

        @pl.when(hit == 1)
        def _():
            place = lax.rem(y - t // per_row + rows, rows) * per_row + lax.rem(t, per_row)
            tile_ref[jnp.minimum(count, tile_ref.shape[0] - 1)] = place

        return count + hit

    lax.fori_loop(0, tiles, one_tile, jnp.int32(0))


def plan(selected, me, ring, per_row, capacity, rows_of_chips):
    smem = pl.BlockSpec(memory_space=pltpu.SMEM)
    return pl.pallas_call(
        functools.partial(plan_kernel, ring, per_row),
        out_shape=(
            jax.ShapeDtypeStruct((capacity,), jnp.int32),
            jax.ShapeDtypeStruct((rows_of_chips * per_row,), jnp.int32),
        ),
        in_specs=[smem, smem],
        out_specs=(smem, smem),
        name="plan",
    )(me, selected)


def row_to_columns(row):
    return jnp.broadcast_to(row, (128, row.shape[1])).T


def pack(out_view, acc, level):
    rows = acc.shape[0]
    largest = jnp.maximum(jnp.max(jnp.abs(acc), axis=1, keepdims=True), 1e-30)
    code = jnp.round(acc * (FULL / largest)).astype(jnp.int32)
    out_view[0:rows, :] = code.astype(jnp.int16)
    lane = lax.broadcasted_iota(jnp.int32, (rows, 128), 1)
    both = jnp.where(lane == 0, level, jnp.log2(largest)).T[0:8, :]
    whole = jnp.round(jnp.clip(both, NONE, -NONE) * FINE).astype(jnp.int32)
    high = whole >> 16
    low = (whole & 0xFFFF) - 32768
    rank = lax.broadcasted_iota(jnp.int32, (8, 128), 0)
    stats = jnp.zeros((8, 128), jnp.int32)
    n = rows // 128
    for k, source in enumerate((high, low)):
        for stat in range(2):
            for g in range(n):
                piece = jnp.broadcast_to(source[stat : stat + 1, g * 128 : (g + 1) * 128], (8, 128))
                stats = jnp.where(rank == (k * 2 + stat) * n + g, piece, stats)
    out_view[rows : rows + 8, :] = stats.astype(jnp.int16)


def unpack_stats(view, rows):
    n = rows // 128
    raw = view[rows : rows + 8, :].astype(jnp.int32)
    found = []
    for stat in range(2):
        high = [raw[stat * n + g : stat * n + g + 1, :] for g in range(n)]
        low = [raw[(2 + stat) * n + g : (2 + stat) * n + g + 1, :] for g in range(n)]
        whole = [(h << 16) + (w + 32768) for h, w in zip(high, low)]
        found.append(jnp.concatenate([w.astype(jnp.float32) for w in whole], axis=1) * (1.0 / FINE))
    return found


def block_kernel(
    factor,
    tile_ref,
    valid_ref,
    q_ref,
    other_ref,
    next_ref,
    kt_ref,
    v_ref,
    *refs,
):
    *out_refs, s0_ref, s1_ref, top_ref, total_ref, acc_ref, held_ref, sem = refs
    i = pl.program_id(0)
    length = kt_ref.shape[1]
    rows = q_ref.shape[2]
    per_row, sides = out_refs[0].shape[0], out_refs[0].shape[1]
    valid = valid_ref[0]
    steps = length // KEYS

    def score(q, s_ref, slot, j):
        s = jnp.dot(q, kt_ref[:, j * KEYS : (j + 1) * KEYS], preferred_element_type=jnp.float32)
        position = lax.broadcasted_iota(jnp.int32, (1, KEYS), 1) + j * KEYS
        s = s + jnp.where(position < valid, 0.0, NEG)
        s_ref[:, j * KEYS : (j + 1) * KEYS] = s
        best = s[:, 0:128]
        for g in range(1, KEYS // 128):
            best = jnp.maximum(best, s[:, g * 128 : (g + 1) * 128])
        if j:
            best = jnp.maximum(best, top_ref[slot])
        if j == steps - 1:
            best = jnp.broadcast_to(jnp.max(best, axis=1, keepdims=True), (rows, 128))
        top_ref[slot] = best

    def weigh(s_ref, slot, j):
        tops = jnp.concatenate([top_ref[slot]] * (KEYS // 128), axis=1)
        p = jnp.exp2((s_ref[:, j * KEYS : (j + 1) * KEYS] - tops) * factor)
        total = p[:, 0:128]
        for g in range(1, KEYS // 128):
            total += p[:, g * 128 : (g + 1) * 128]
        product = jnp.dot(
            p.astype(jnp.bfloat16), v_ref[j * KEYS : (j + 1) * KEYS, :], preferred_element_type=jnp.float32
        )
        total_ref[...] = total_ref[...] + total if j else total
        acc_ref[...] = acc_ref[...] + product if j else product

    def send(slot, place):
        row = lax.rem(len(out_refs) - place // per_row, len(out_refs))
        for r, ref in enumerate(out_refs):

            @pl.when(row == r)
            def _():
                pltpu.make_async_copy(held_ref.at[slot], ref.at[lax.rem(place, per_row)], sem.at[slot]).start()

    def settle(slot):
        pltpu.make_async_copy(held_ref.at[slot], out_refs[0].at[0], sem.at[slot]).wait()

    def finish(slot):
        total = jnp.sum(total_ref[...], axis=1, keepdims=True)
        level = top_ref[slot][:, 0:1] * factor + jnp.log2(total)
        level = jnp.where(valid > 0, level, NONE)
        value = acc_ref[...] / total

        @pl.when(i > 0)
        def _():
            settle(slot)

        part = rows // sides
        for side in range(sides):
            here = slice(side * part, (side + 1) * part)
            pack(held_ref.at[slot, side], value[here], level[here])
        send(slot, tile_ref[2 * i + slot])

    @pl.when(i == 0)
    def _():
        for j in range(steps):
            score(q_ref[0, 0], s0_ref, 0, j)

    for j in range(steps):
        score(other_ref[0, 0], s1_ref, 1, j)
        weigh(s0_ref, 0, j)
    finish(0)
    for j in range(steps):
        score(next_ref[0, 0], s0_ref, 0, j)
        weigh(s1_ref, 1, j)
    finish(1)

    @pl.when(i == pl.num_programs(0) - 1)
    def _():
        for slot in range(2):
            settle(slot)


def block_part(factor, sides, tile_ids, valid, q, kt, v):
    tile_rows, per_row, rows, _ = q.shape
    capacity = tile_ids.shape[0]

    def tile_block(ahead):
        def index(i, t, n):
            tile = t[jnp.minimum(2 * i + ahead, capacity - 1)]
            return (tile // per_row, lax.rem(tile, per_row), 0, 0)

        return pl.BlockSpec((1, 1, rows, 128), index)

    padded = rows // sides + 8
    return pl.pallas_call(
        functools.partial(block_kernel, factor),
        out_shape=(jax.ShapeDtypeStruct((per_row, sides, padded, 128), jnp.int16),) * tile_rows,
        grid_spec=pltpu.PrefetchScalarGridSpec(
            num_scalar_prefetch=2,
            grid=(capacity // 2,),
            in_specs=[
                tile_block(0),
                tile_block(1),
                tile_block(2),
                pl.BlockSpec(kt.shape, lambda i, t, n: (0, 0)),
                pl.BlockSpec(v.shape, lambda i, t, n: (0, 0)),
            ],
            out_specs=(pl.BlockSpec(memory_space=pl.ANY),) * tile_rows,
            scratch_shapes=[
                pltpu.VMEM((rows, kt.shape[1]), jnp.float32),
                pltpu.VMEM((rows, kt.shape[1]), jnp.float32),
                pltpu.VMEM((2, rows, 128), jnp.float32),
                pltpu.VMEM((rows, 128), jnp.float32),
                pltpu.VMEM((rows, 128), jnp.float32),
                pltpu.VMEM((2, sides, padded, 128), jnp.int16),
                pltpu.SemaphoreType.DMA((2,)),
            ],
        ),
        name="block_part",
    )(tile_ids, valid, q, q, q, kt, v)


def fresh_kernel(factor, ring, tokens, me_ref, q_ref, k_ref, v_ref, out_ref):
    k = pl.program_id(0)
    per_row = pl.num_programs(0)
    y, z = me_ref[0], me_ref[1]
    rows = q_ref.shape[1]
    sides = out_ref.shape[1]
    part = rows // sides
    keys = k_ref.shape[0]
    s = lax.dot_general(q_ref[0], k_ref[...], (((1,), (1,)), ((), ())), preferred_element_type=jnp.float32)
    row = lax.broadcasted_iota(jnp.int32, (rows, 128), 0)
    lane = lax.broadcasted_iota(jnp.int32, (1, keys), 1)
    here = (y * ring + k * sides + row // part) * tokens + lax.rem(row, tokens)
    rows_of_chips = keys // tokens
    source = lax.rem(y - lane // tokens + rows_of_chips, rows_of_chips)
    there = (source * ring + z) * tokens + lax.rem(lane, tokens)
    allowed = there <= jnp.concatenate([here] * (keys // 128), axis=1)
    top = jnp.max(jnp.where(allowed, s, NEG), axis=1, keepdims=True)
    p = jnp.where(allowed, jnp.exp2((s - top) * factor), 0.0)
    high = p.astype(jnp.bfloat16)
    low = (p - high.astype(jnp.float32)).astype(jnp.bfloat16)
    acc = jnp.dot(high, v_ref[...], preferred_element_type=jnp.float32) + jnp.dot(
        low, v_ref[...], preferred_element_type=jnp.float32
    )
    total = jnp.maximum(jnp.sum(p, axis=1, keepdims=True), 1e-30)
    level = jnp.maximum(top * factor + jnp.log2(total), NONE)
    value = acc / total
    for side in range(sides):
        here = slice(side * part, (side + 1) * part)
        pack(out_ref.at[0, side], value[here], level[here])


def fresh_part(factor, ring, tokens, sides, me, q, k, v):
    per_row, rows, _ = q.shape
    padded = rows // sides + 8
    return pl.pallas_call(
        functools.partial(fresh_kernel, factor, ring, tokens),
        out_shape=jax.ShapeDtypeStruct((per_row, sides, padded, 128), jnp.int16),
        grid_spec=pltpu.PrefetchScalarGridSpec(
            num_scalar_prefetch=1,
            grid=(per_row,),
            in_specs=[
                pl.BlockSpec((1, rows, 128), lambda i, m: (i, 0, 0)),
                pl.BlockSpec(k.shape, lambda i, m: (0, 0)),
                pl.BlockSpec(v.shape, lambda i, m: (0, 0)),
            ],
            out_specs=pl.BlockSpec((1, sides, padded, 128), lambda i, m: (i, 0, 0, 0)),
        ),
        name="fresh_part",
    )(me, q, k, v)


def column_kernel(flag_ref, *refs):
    k = pl.program_id(0)
    per_row = pl.num_programs(0)
    *part_refs, out_ref = refs
    sources = len(part_refs) - 1
    _, sides, padded, _ = part_refs[0].shape
    rows = padded - 8
    for side in range(sides):
        views = [ref.at[0, side] for ref in part_refs]
        stats = []
        for sy, view in enumerate(views):
            level, largest = unpack_stats(view, rows)
            if sy < sources:
                taken = flag_ref[sy * per_row + k] == 1
                level = jnp.where(taken, level, NONE)
                largest = jnp.where(taken, largest, 0.0)
            stats.append((level, largest))
        top = functools.reduce(jnp.maximum, [level for level, _ in stats])
        weights = [jnp.exp2(level - top) for level, _ in stats]
        total = functools.reduce(jnp.add, weights)
        acc = jnp.zeros((rows, 128), jnp.float32)
        for view, weight, (_, largest) in zip(views, weights, stats):
            share = row_to_columns(weight * jnp.exp2(largest) / (FULL * total))
            acc += view[0:rows, :].astype(jnp.int32).astype(jnp.float32) * share
        level = jnp.maximum(top + jnp.log2(total), NONE)
        pack(out_ref.at[side], acc, row_to_columns(level)[:, 0:1])


def column_part(flags, got, fresh):
    per_row, sides, padded, _ = fresh.shape
    part = pl.BlockSpec((1, sides, padded, 128), lambda i, f: (i, 0, 0, 0))
    return pl.pallas_call(
        column_kernel,
        out_shape=jax.ShapeDtypeStruct((per_row * sides, padded, 128), jnp.int16),
        grid_spec=pltpu.PrefetchScalarGridSpec(
            num_scalar_prefetch=1,
            grid=(per_row,),
            in_specs=[part] * (len(got) + 1),
            out_specs=pl.BlockSpec((sides, padded, 128), lambda i, f: (i, 0, 0)),
        ),
        name="column_part",
    )(flags, *got, fresh)


def ring_kernel(got_ref, out_ref):
    sources, padded, _ = got_ref.shape
    rows = padded - 8
    stats = [unpack_stats(got_ref.at[s], rows) for s in range(sources)]
    top = functools.reduce(jnp.maximum, [level for level, _ in stats])
    weights = [jnp.exp2(level - top) for level, _ in stats]
    total = functools.reduce(jnp.add, weights)
    acc = jnp.zeros((rows, 128), jnp.float32)
    for s in range(sources):
        share = row_to_columns(weights[s] * jnp.exp2(stats[s][1]) / (FULL * total))
        acc += got_ref[s, 0:rows, :].astype(jnp.int32).astype(jnp.float32) * share
    out_ref[...] = acc.astype(jnp.bfloat16)


def ring_part(got):
    vmem = pl.BlockSpec(memory_space=pltpu.VMEM)
    return pl.pallas_call(
        ring_kernel,
        out_shape=jax.ShapeDtypeStruct((got.shape[1] - 8, 128), jnp.bfloat16),
        in_specs=[vmem],
        out_specs=vmem,
        name="ring_part",
    )(got)


def shards(queries, fresh_keys, fresh_values, cache_keys, cache_values, selected, start):
    part, q_heads, head_size = queries.shape
    kv_heads = fresh_keys.shape[1]
    group = q_heads // kv_heads
    heads_axis = lax.axis_size("head")
    ctx_size = lax.axis_size("ctx")
    ctx_index = lax.axis_index("ctx")
    ring = RING
    columns = ctx_size // ring
    along = [[y * ring + z for z in range(ring)] for y in range(columns)]
    tokens = part * heads_axis
    sides = TILE // tokens
    per_row = ring // sides
    tiles, sel = selected.shape
    capacity = tiles * sel // ctx_size
    factor = head_size**-0.5 * math.log2(math.e)
    length = cache_keys.shape[0]

    mixed = jnp.concatenate(
        [
            queries.reshape(part, kv_heads, group, head_size),
            fresh_keys[:, :, None],
            fresh_values[:, :, None],
        ],
        axis=2,
    ).transpose(1, 2, 0, 3)
    mixed = lax.all_to_all(mixed, "head", split_axis=0, concat_axis=0, tiled=True)
    mixed = mixed.transpose(1, 0, 2, 3).reshape(group + 2, tokens, head_size)

    def exchange(x):
        return lax.all_to_all(
            x, "ctx", split_axis=0, concat_axis=0, tiled=True, axis_index_groups=along
        )

    def shift(x, by):
        pairs = [
            (y * ring + z, (y + by) % columns * ring + z) for y in range(columns) for z in range(ring)
        ]
        return lax.ppermute(x, "ctx", pairs)

    def shifts(x):
        return [x] + [shift(x, by) for by in range(1, columns)]

    me = jnp.stack([ctx_index // ring, ctx_index % ring])
    kt = cache_keys[:, 0].T
    v = cache_values[:, 0]
    tile_ids, flags = plan(selected, ctx_index.reshape(1), ring, per_row, capacity, columns)
    valid = jnp.clip(start - ctx_index * length, 0, length)

    heads = group // CHUNKS
    row_q = [
        exchange(
            jnp.broadcast_to(
                mixed[None, c * heads : (c + 1) * heads], (ring, heads, tokens, head_size)
            )
        ).reshape(per_row, sides * heads * tokens, head_size)
        for c in range(CHUNKS)
    ]
    all_q = [jnp.stack(shifts(q)) for q in row_q]
    column = jnp.stack(shifts(mixed[group:]))
    column_k = column[:, 0].reshape(columns * tokens, head_size)
    column_v = column[:, 1].reshape(columns * tokens, head_size)
    sent = [block_part(factor, sides, tile_ids, valid, q, kt, v) for q in all_q]
    got = [[x[0]] + [shift(x[by], by) for by in range(1, columns)] for x in sent]
    fresh = [fresh_part(factor, ring, tokens, sides, me, q, column_k, column_v) for q in row_q]
    sent = [column_part(flags, x, f) for x, f in zip(got, fresh)]
    got = [exchange(x) for x in sent]
    result = jnp.concatenate([ring_part(x) for x in got], axis=0)
    result = result.reshape(group, heads_axis, part, head_size).transpose(1, 0, 2, 3)
    result = lax.all_to_all(result, "head", split_axis=0, concat_axis=0, tiled=True)
    return result.reshape(q_heads, part, head_size).transpose(1, 0, 2)


def solution(mesh):
    in_specs = (
        P(("ctx", "head"), None, None),
        P(("ctx", "head"), None, None),
        P(("ctx", "head"), None, None),
        P("ctx", "head", None),
        P("ctx", "head", None),
        P(),
        P(),
    )
    out_specs = P(("ctx", "head"), None, None)
    return jax.shard_map(shards, mesh=mesh, in_specs=in_specs, out_specs=out_specs, check_vma=False)
```

```python
import functools
import math

import jax
import jax.numpy as jnp
from jax import lax
from jax.experimental import pallas as pl
from jax.experimental.pallas import tpu as pltpu
from jax.sharding import PartitionSpec as P

TILE = 128
RING = 16
NEAR = 4
KEYS = 512
NEG = -1e30
NONE = -4000.0
FINE = 2.0**19
FULL = 32767.0


def plan_kernel(ring, per_row, slots, me_ref, sel_ref, place_ref, slot_ref, over_ref, count_ref):
    tiles, sel = sel_ref.shape
    capacity = place_ref.shape[0]
    rows = slot_ref.shape[0] // per_row
    me = me_ref[0]
    y, z = me // ring, lax.rem(me, ring)
    for i in range(capacity):
        place_ref[i] = 0
    for i in range(slot_ref.shape[0]):
        slot_ref[i] = -1

    def clear(i, _):
        count_ref[i] = 0
        return 0

    lax.fori_loop(0, count_ref.shape[0], clear, 0)

    def one_tile(t, carry):
        count, most = carry
        row, k = t // per_row, lax.rem(t, per_row)
        hit = jnp.int32(-1)
        for i in range(sel):
            b = sel_ref[t, i]
            slot = count_ref[b * rows + row]
            count_ref[b * rows + row] = slot + 1
            most = jnp.maximum(most, slot + 1)
            hit = jnp.where(b == me, slot, hit)

            @pl.when((row == y) & (lax.rem(b, ring) == z))
            def _():
                slot_ref[(b // ring) * per_row + k] = slot

        @pl.when(hit >= 0)
        def _():
            place_ref[jnp.minimum(count, capacity - 1)] = row * capacity + hit

        return count + jnp.where(hit >= 0, 1, 0), most

    _, most = lax.fori_loop(0, tiles, one_tile, (jnp.int32(0), jnp.int32(0)))
    over_ref[0] = jnp.where(most > slots, 1, 0)


def plan(selected, me, ring, per_row, slots, capacity, rows_of_chips):
    smem = pl.BlockSpec(memory_space=pltpu.SMEM)
    return pl.pallas_call(
        functools.partial(plan_kernel, ring, per_row, slots),
        out_shape=(
            jax.ShapeDtypeStruct((capacity,), jnp.int32),
            jax.ShapeDtypeStruct((rows_of_chips * per_row,), jnp.int32),
            jax.ShapeDtypeStruct((1,), jnp.int32),
        ),
        in_specs=[smem, smem],
        out_specs=(smem, smem, smem),
        scratch_shapes=[pltpu.SMEM((ring * rows_of_chips * rows_of_chips,), jnp.int32)],
        name="plan",
    )(me, selected)


def gather_kernel(slots, slot_ref, q_ref, kv_ref, first_ref, rest_ref, sem, kv_sem):
    near, sides, far, rows, _ = q_ref.shape
    columns = first_ref.shape[0]
    per_row = near * far
    tail = first_ref.shape[1] - kv_ref.shape[0]

    def tile(c, k, side, ref, slot):
        start = pl.multiple_of((slot * sides + side) * rows, rows)
        return pltpu.make_async_copy(
            q_ref.at[lax.rem(k, near), side, k // near],
            ref.at[c, pl.ds(start, rows)],
            sem.at[c * per_row + k, side],
        )

    def each(act):
        def one(i, _):
            c, k = i // per_row, lax.rem(i, per_row)
            slot = slot_ref[i]
            for side in range(sides):

                @pl.when((slot >= 0) & (slot < slots))
                def _():
                    act(tile(c, k, side, first_ref, slot))

                @pl.when(slot >= slots)
                def _():
                    act(tile(c, k, side, rest_ref, slot - slots))

            return 0

        lax.fori_loop(0, columns * per_row, one, 0)
        for c in range(columns):
            act(
                pltpu.make_async_copy(
                    kv_ref, first_ref.at[c, tail : tail + kv_ref.shape[0]], kv_sem.at[c]
                )
            )

    each(lambda copy: copy.start())
    each(lambda copy: copy.wait())


def gather_tiles(slots, capacity, slot, q, kv, columns):
    near, sides, far, rows, _ = q.shape
    full = sides * rows
    anywhere = pl.BlockSpec(memory_space=pl.ANY)
    return pl.pallas_call(
        functools.partial(gather_kernel, slots),
        out_shape=(
            jax.ShapeDtypeStruct((columns, slots * full + kv.shape[0], 128), q.dtype),
            jax.ShapeDtypeStruct((columns, (capacity - slots) * full, 128), q.dtype),
        ),
        in_specs=[pl.BlockSpec(memory_space=pltpu.SMEM), anywhere, anywhere],
        out_specs=(anywhere, anywhere),
        scratch_shapes=[
            pltpu.SemaphoreType.DMA((columns * near * far, sides)),
            pltpu.SemaphoreType.DMA((columns,)),
        ],
        name="gather_tiles",
    )(slot, q, kv)


def row_to_columns(row):
    return jnp.broadcast_to(row, (128, row.shape[1])).T


def pack(out_view, acc, level):
    rows = acc.shape[0]
    largest = jnp.maximum(jnp.max(jnp.abs(acc), axis=1, keepdims=True), 1e-30)
    code = jnp.round(acc * (FULL / largest)).astype(jnp.int32)
    out_view[0:rows, :] = code.astype(jnp.int16)
    lane = lax.broadcasted_iota(jnp.int32, (rows, 128), 1)
    both = jnp.where(lane == 0, level, jnp.log2(largest)).T[0:8, :]
    whole = jnp.round(jnp.clip(both, NONE, -NONE) * FINE).astype(jnp.int32)
    high = whole >> 16
    low = (whole & 0xFFFF) - 32768
    rank = lax.broadcasted_iota(jnp.int32, (8, 128), 0)
    stats = jnp.zeros((8, 128), jnp.int32)
    n = rows // 128
    for k, source in enumerate((high, low)):
        for stat in range(2):
            for g in range(n):
                piece = jnp.broadcast_to(source[stat : stat + 1, g * 128 : (g + 1) * 128], (8, 128))
                stats = jnp.where(rank == (k * 2 + stat) * n + g, piece, stats)
    out_view[rows : rows + 8, :] = stats.astype(jnp.int16)


def unpack_stats(view, rows):
    n = rows // 128
    raw = view[rows : rows + 8, :].astype(jnp.int32)
    found = []
    for stat in range(2):
        high = [raw[stat * n + g : stat * n + g + 1, :] for g in range(n)]
        low = [raw[(2 + stat) * n + g : (2 + stat) * n + g + 1, :] for g in range(n)]
        whole = [(h << 16) + (w + 32768) for h, w in zip(high, low)]
        found.append(jnp.concatenate([w.astype(jnp.float32) for w in whole], axis=1) * (1.0 / FINE))
    return found


def block_kernel(
    factor,
    slots,
    place_ref,
    valid_ref,
    q_ref,
    rest_ref,
    next_ref,
    next_rest_ref,
    kt_ref,
    v_ref,
    out_ref,
    out_rest_ref,
    s0_ref,
    s1_ref,
    top_ref,
    total_ref,
    acc_ref,
    held_ref,
    sem,
):
    i = pl.program_id(0)
    last = pl.num_programs(0) - 1
    length = kt_ref.shape[1]
    rows = q_ref.shape[1] // 2
    valid = valid_ref[0]
    steps = length // KEYS
    capacity = slots + out_rest_ref.shape[1]

    def score(q, s_ref, slot, j):
        s = jnp.dot(q, kt_ref[:, j * KEYS : (j + 1) * KEYS], preferred_element_type=jnp.float32)
        position = lax.broadcasted_iota(jnp.int32, (1, KEYS), 1) + j * KEYS
        s = s + jnp.where(position < valid, 0.0, NEG)
        s_ref[:, j * KEYS : (j + 1) * KEYS] = s
        best = s[:, 0:128]
        for g in range(1, KEYS // 128):
            best = jnp.maximum(best, s[:, g * 128 : (g + 1) * 128])
        if j:
            best = jnp.maximum(best, top_ref[slot])
        if j == steps - 1:
            best = jnp.broadcast_to(jnp.max(best, axis=1, keepdims=True), (rows, 128))
        top_ref[slot] = best

    def weigh(s_ref, slot, j):
        tops = jnp.concatenate([top_ref[slot]] * (KEYS // 128), axis=1)
        p = jnp.exp2((s_ref[:, j * KEYS : (j + 1) * KEYS] - tops) * factor)
        total = p[:, 0:128]
        for g in range(1, KEYS // 128):
            total += p[:, g * 128 : (g + 1) * 128]
        product = jnp.dot(
            p.astype(jnp.bfloat16), v_ref[j * KEYS : (j + 1) * KEYS, :], preferred_element_type=jnp.float32
        )
        total_ref[...] = total_ref[...] + total if j else total
        acc_ref[...] = acc_ref[...] + product if j else product

    def each_target(step, act):
        place = place_ref[step]
        row, slot = place // capacity, lax.rem(place, capacity)

        @pl.when(slot < slots)
        def _():
            act(pltpu.make_async_copy(held_ref, out_ref.at[row, slot], sem))

        @pl.when(slot >= slots)
        def _():
            act(pltpu.make_async_copy(held_ref, out_rest_ref.at[row, slot - slots], sem))

    def finish(side):
        total = jnp.sum(total_ref[...], axis=1, keepdims=True)
        level = top_ref[side][:, 0:1] * factor + jnp.log2(total)
        level = jnp.where(valid > 0, level, NONE)
        pack(held_ref.at[side], acc_ref[...] / total, level)

    def choose(step, ref, other, side):
        rest = lax.rem(place_ref[step], capacity) >= slots
        here = slice(side * rows, (side + 1) * rows)
        return jnp.where(rest, other[0, here, :], ref[0, here, :])

    @pl.when(i == 0)
    def _():
        q = choose(i, q_ref, rest_ref, 0)
        for j in range(steps):
            score(q, s0_ref, 0, j)

    q = choose(i, q_ref, rest_ref, 1)
    for j in range(steps):
        score(q, s1_ref, 1, j)
        weigh(s0_ref, 0, j)

    @pl.when(i > 0)
    def _():
        each_target(i - 1, lambda copy: copy.wait())

    finish(0)
    q = choose(jnp.minimum(i + 1, last), next_ref, next_rest_ref, 0)
    for j in range(steps):
        score(q, s0_ref, 0, j)
        weigh(s1_ref, 1, j)
    finish(1)
    each_target(i, lambda copy: copy.start())

    @pl.when(i == last)
    def _():
        each_target(i, lambda copy: copy.wait())


def block_part(factor, slots, sides, full, place, valid, q, rest, kt, v):
    columns = q.shape[0]
    capacity = place.shape[0]
    extra = capacity - slots
    rows = full // sides

    def tiles(ahead, first):
        def index(i, t, n):
            at = t[jnp.minimum(i + ahead, capacity - 1)]
            row, slot = at // capacity, lax.rem(at, capacity)
            slot = jnp.minimum(slot, slots - 1) if first else jnp.maximum(slot - slots, 0)
            return (row, slot, 0)

        return pl.BlockSpec((1, full, 128), index)

    anywhere = pl.BlockSpec(memory_space=pl.ANY)
    return pl.pallas_call(
        functools.partial(block_kernel, factor, slots),
        out_shape=(
            jax.ShapeDtypeStruct((columns, slots, sides, rows + 8, 128), jnp.int16),
            jax.ShapeDtypeStruct((columns, extra, sides, rows + 8, 128), jnp.int16),
        ),
        grid_spec=pltpu.PrefetchScalarGridSpec(
            num_scalar_prefetch=2,
            grid=(capacity,),
            in_specs=[
                tiles(0, True),
                tiles(0, False),
                tiles(1, True),
                tiles(1, False),
                pl.BlockSpec(kt.shape, lambda i, t, n: (0, 0)),
                pl.BlockSpec(v.shape, lambda i, t, n: (0, 0)),
            ],
            out_specs=(anywhere, anywhere),
            scratch_shapes=[
                pltpu.VMEM((rows, kt.shape[1]), jnp.float32),
                pltpu.VMEM((rows, kt.shape[1]), jnp.float32),
                pltpu.VMEM((2, rows, 128), jnp.float32),
                pltpu.VMEM((rows, 128), jnp.float32),
                pltpu.VMEM((rows, 128), jnp.float32),
                pltpu.VMEM((sides, rows + 8, 128), jnp.int16),
                pltpu.SemaphoreType.DMA,
            ],
        ),
        name="block_part",
    )(place, valid, q, rest, q, rest, kt, v)


def fresh_kernel(factor, ring, tokens, me_ref, q_ref, k_ref, v_ref, value_ref, level_ref):
    k = pl.program_id(0)
    y, z = me_ref[0], me_ref[1]
    _, sides, _, rows, _ = q_ref.shape
    keys = k_ref.shape[0]
    row = lax.broadcasted_iota(jnp.int32, (rows, 128), 0)
    lane = lax.broadcasted_iota(jnp.int32, (1, keys), 1)
    there = (lane // tokens * ring + z) * tokens + lax.rem(lane, tokens)
    for side in range(sides):
        s = lax.dot_general(
            q_ref[0, side, 0], k_ref[...], (((1,), (1,)), ((), ())), preferred_element_type=jnp.float32
        )
        here = (y * ring + k * sides + side) * tokens + lax.rem(row, tokens)
        allowed = there <= jnp.concatenate([here] * (keys // 128), axis=1)
        top = jnp.max(jnp.where(allowed, s, NEG), axis=1, keepdims=True)
        p = jnp.where(allowed, jnp.exp2((s - top) * factor), 0.0)
        high = p.astype(jnp.bfloat16)
        low = (p - high.astype(jnp.float32)).astype(jnp.bfloat16)
        acc = jnp.dot(high, v_ref[...], preferred_element_type=jnp.float32) + jnp.dot(
            low, v_ref[...], preferred_element_type=jnp.float32
        )
        total = jnp.maximum(jnp.sum(p, axis=1, keepdims=True), 1e-30)
        level = jnp.maximum(top * factor + jnp.log2(total), NONE)
        value_ref[0, side] = acc / total
        level_ref[0, side] = jnp.broadcast_to(level, (rows, 128))


def fresh_part(factor, ring, tokens, me, q, k, v):
    near, sides, far, rows, _ = q.shape
    per_row = near * far
    wide = jax.ShapeDtypeStruct((per_row, sides, rows, 128), jnp.float32)
    block = pl.BlockSpec((1, sides, rows, 128), lambda i, m: (i, 0, 0, 0))
    return pl.pallas_call(
        functools.partial(fresh_kernel, factor, ring, tokens),
        out_shape=(wide, wide),
        grid_spec=pltpu.PrefetchScalarGridSpec(
            num_scalar_prefetch=1,
            grid=(per_row,),
            in_specs=[
                pl.BlockSpec((1, sides, 1, rows, 128), lambda i, m: (lax.rem(i, near), 0, i // near, 0, 0)),
                pl.BlockSpec(k.shape, lambda i, m: (0, 0)),
                pl.BlockSpec(v.shape, lambda i, m: (0, 0)),
            ],
            out_specs=(block, block),
        ),
        name="fresh_part",
    )(me, q, k, v)


def column_kernel(slots, slot_ref, *refs):
    *part_refs, value_ref, level_ref, out_ref, acc_ref, top_ref, total_ref = refs
    k = pl.program_id(0)
    per_row = pl.num_programs(0)
    sources = len(part_refs) // 2
    _, sides, rows, _ = value_ref.shape
    for side in range(sides):
        acc_ref[side] = value_ref[0, side]
        top_ref[side] = level_ref[0, side]
        total_ref[side] = jnp.ones((rows, 128), jnp.float32)

    def add(ref):
        for side in range(sides):
            view = ref.at[0, 0, side]
            level, largest = unpack_stats(view, rows)
            level = row_to_columns(level)
            size = row_to_columns(jnp.exp2(largest) * (1.0 / FULL))
            old = top_ref[side]
            new = jnp.maximum(old, level)
            shrink = jnp.exp2(old - new)
            weight = jnp.exp2(level - new)
            value = view[0:rows, :].astype(jnp.int32).astype(jnp.float32)
            acc_ref[side] = acc_ref[side] * shrink + value * (weight * size)
            total_ref[side] = total_ref[side] * shrink + weight
            top_ref[side] = new

    for c in range(sources):
        slot = slot_ref[c * per_row + k]
        pl.when((slot >= 0) & (slot < slots))(functools.partial(add, part_refs[2 * c]))
        pl.when(slot >= slots)(functools.partial(add, part_refs[2 * c + 1]))

    for side in range(sides):
        total = total_ref[side]
        level = jnp.maximum(top_ref[side] + jnp.log2(total), NONE)[:, 0:1]
        pack(out_ref.at[0, side, 0], acc_ref[side] / total, level)


def column_part(slots, near, far, slot, got, rest, value, level):
    columns, _, sides, padded, _ = got.shape
    per_row = near * far
    rows = padded - 8

    def source(c, first):
        def index(i, t):
            at = t[c * per_row + i]
            return (c, jnp.clip(at, 0, slots - 1) if first else jnp.maximum(at - slots, 0), 0, 0, 0)

        return pl.BlockSpec((1, 1, sides, padded, 128), index)

    wide = pl.BlockSpec((1, sides, rows, 128), lambda i, t: (i, 0, 0, 0))
    return pl.pallas_call(
        functools.partial(column_kernel, slots),
        out_shape=jax.ShapeDtypeStruct((near, sides, far, padded, 128), jnp.int16),
        grid_spec=pltpu.PrefetchScalarGridSpec(
            num_scalar_prefetch=1,
            grid=(per_row,),
            in_specs=[source(c, first) for c in range(columns) for first in (True, False)] + [wide, wide],
            out_specs=pl.BlockSpec((1, sides, 1, padded, 128), lambda i, t: (lax.rem(i, near), 0, i // near, 0, 0)),
            scratch_shapes=[pltpu.VMEM((sides, rows, 128), jnp.float32)] * 3,
        ),
        name="column_part",
    )(slot, *[x for c in range(columns) for x in (got, rest)], value, level)


def joined(views, rows):
    stats = [unpack_stats(view, rows) for view in views]
    top = functools.reduce(jnp.maximum, [level for level, _ in stats])
    weights = [jnp.exp2(level - top) for level, _ in stats]
    total = functools.reduce(jnp.add, weights)
    acc = jnp.zeros((rows, 128), jnp.float32)
    for view, weight, (_, largest) in zip(views, weights, stats):
        share = row_to_columns(weight * jnp.exp2(largest) / (FULL * total))
        acc += view[0:rows, :].astype(jnp.int32).astype(jnp.float32) * share
    return acc, top + jnp.log2(total)


def near_kernel(got_ref, out_ref):
    sources, _, padded, _ = got_ref.shape
    acc, level = joined([got_ref.at[s, 0] for s in range(sources)], padded - 8)
    pack(out_ref.at[0], acc, row_to_columns(jnp.maximum(level, NONE))[:, 0:1])


def near_part(got):
    sources, places, padded, _ = got.shape
    return pl.pallas_call(
        near_kernel,
        out_shape=jax.ShapeDtypeStruct((places, padded, 128), jnp.int16),
        grid=(places,),
        in_specs=[pl.BlockSpec((sources, 1, padded, 128), lambda i: (0, i, 0, 0))],
        out_specs=pl.BlockSpec((1, padded, 128), lambda i: (i, 0, 0)),
        name="near_part",
    )(got)


def far_kernel(got_ref, out_ref):
    sources, padded, _ = got_ref.shape
    acc, _ = joined([got_ref.at[s] for s in range(sources)], padded - 8)
    out_ref[...] = acc.astype(jnp.bfloat16)


def far_part(got):
    vmem = pl.BlockSpec(memory_space=pltpu.VMEM)
    return pl.pallas_call(
        far_kernel,
        out_shape=jax.ShapeDtypeStruct((got.shape[1] - 8, 128), jnp.bfloat16),
        in_specs=[vmem],
        out_specs=vmem,
        name="far_part",
    )(got)


def shards(queries, fresh_keys, fresh_values, cache_keys, cache_values, selected, start):
    part, q_heads, head_size = queries.shape
    kv_heads = fresh_keys.shape[1]
    group = q_heads // kv_heads
    heads_axis = lax.axis_size("head")
    ctx_size = lax.axis_size("ctx")
    ctx_index = lax.axis_index("ctx")
    ring, near = RING, NEAR
    far = ring // near
    columns = ctx_size // ring
    across = [[y * ring + z for y in range(columns)] for z in range(ring)]
    close = [[y * ring + a * near + b for b in range(near)] for y in range(columns) for a in range(far)]
    wide = [[y * ring + a * near + b for a in range(far)] for y in range(columns) for b in range(near)]
    tokens = part * heads_axis
    sides = TILE // tokens
    per_row = ring // sides
    tiles, sel = selected.shape
    capacity = tiles * sel // ctx_size
    factor = head_size**-0.5 * math.log2(math.e)
    length = cache_keys.shape[0]

    mixed = jnp.concatenate(
        [
            queries.reshape(part, kv_heads, group, head_size),
            fresh_keys[:, :, None],
            fresh_values[:, :, None],
        ],
        axis=2,
    ).transpose(1, 2, 0, 3)
    mixed = lax.all_to_all(mixed, "head", split_axis=0, concat_axis=0, tiled=True)
    mixed = mixed.transpose(1, 0, 2, 3).reshape(group + 2, tokens, head_size)

    def exchange(x, groups):
        return lax.all_to_all(
            x, "ctx", split_axis=0, concat_axis=0, tiled=True, axis_index_groups=groups
        )

    def copies(x, n):
        return jnp.broadcast_to(x[None], (n,) + x.shape)

    me = jnp.stack([ctx_index // ring, ctx_index % ring])
    kt = cache_keys[:, 0].T
    v = cache_values[:, 0]
    slots = max(1, capacity - 1)
    place, slot, over = plan(selected, ctx_index.reshape(1), ring, per_row, slots, capacity, columns)
    valid = jnp.clip(start - ctx_index * length, 0, length)
    rows = group * tokens
    places = near // sides

    def rarely(x):
        return lax.cond(over[0] > 0, lambda a: exchange(a, across), lambda a: a, x)

    q = exchange(copies(mixed[:group].reshape(rows, head_size), far), wide)
    q = exchange(copies(q, near), close)
    q = q.reshape(places, sides, far, rows, head_size)
    first, rest = gather_tiles(
        slots, capacity, slot, q, mixed[group:].reshape(2 * tokens, head_size), columns
    )
    first, rest = lax.optimization_barrier((exchange(first, across), rest))
    rest = rarely(rest)
    column = first[:, -2 * tokens :].reshape(columns, 2, tokens, head_size)
    column_k = column[:, 0].reshape(columns * tokens, head_size)
    column_v = column[:, 1].reshape(columns * tokens, head_size)

    sent, sent_rest = block_part(factor, slots, sides, sides * rows, place, valid, first, rest, kt, v)
    got, sent_rest = lax.optimization_barrier((exchange(sent, across), sent_rest))
    got_rest = rarely(sent_rest)
    value, level = fresh_part(factor, ring, tokens, me, q, column_k, column_v)
    sent = column_part(slots, places, far, slot, got, got_rest, value, level)
    got = exchange(sent.reshape(near, far, rows + 8, head_size), close)
    got = exchange(near_part(got), wide)
    result = far_part(got)
    result = result.reshape(group, heads_axis, part, head_size).transpose(1, 0, 2, 3)
    result = lax.all_to_all(result, "head", split_axis=0, concat_axis=0, tiled=True)
    return result.reshape(q_heads, part, head_size).transpose(1, 0, 2)


def solution(mesh):
    in_specs = (
        P(("ctx", "head"), None, None),
        P(("ctx", "head"), None, None),
        P(("ctx", "head"), None, None),
        P("ctx", "head", None),
        P("ctx", "head", None),
        P(),
        P(),
    )
    out_specs = P(("ctx", "head"), None, None)
    return jax.shard_map(shards, mesh=mesh, in_specs=in_specs, out_specs=out_specs, check_vma=False)
```

```python
import functools
import math

import jax
import jax.numpy as jnp
from jax import lax
from jax.experimental import pallas as pl
from jax.experimental.pallas import tpu as pltpu
from jax.sharding import PartitionSpec as P

TILE = 128
RING = 16
KEYS = 512
NEG = -1e30
NONE = -4000.0
FINE = 2.0**19
FULL = 32767.0


def plan_kernel(ring, per_row, cut, me_ref, sel_ref, place_ref, slot_ref, split_ref, over_ref, count_ref):
    tiles, sel = sel_ref.shape
    capacity = place_ref.shape[0]
    rows = slot_ref.shape[0] // per_row
    me = me_ref[0]
    y, z = me // ring, lax.rem(me, ring)
    for i in range(capacity):
        place_ref[i] = 0
    for i in range(slot_ref.shape[0]):
        slot_ref[i] = -1

    def clear(i, _):
        count_ref[i] = 0
        return 0

    lax.fori_loop(0, count_ref.shape[0], clear, 0)

    def one_tile(t, carry):
        front, back, most = carry
        row, k = t // per_row, lax.rem(t, per_row)
        hit = jnp.int32(-1)
        for i in range(sel):
            b = sel_ref[t, i]
            slot = count_ref[b * rows + row]
            count_ref[b * rows + row] = slot + 1
            most = jnp.maximum(most, slot + 1)
            hit = jnp.where(b == me, slot, hit)

            @pl.when((row == y) & (lax.rem(b, ring) == z))
            def _():
                slot_ref[(b // ring) * per_row + k] = slot

        early = (hit >= 0) & (hit < cut)

        @pl.when(hit >= 0)
        def _():
            at = jnp.where(early, jnp.minimum(front, capacity - 1), jnp.maximum(back, 0))
            place_ref[at] = row * capacity + hit

        front = front + jnp.where(early, 1, 0)
        back = back - jnp.where(hit >= cut, 1, 0)
        return front, back, most

    start = (jnp.int32(0), jnp.int32(capacity - 1), jnp.int32(0))
    front, _, most = lax.fori_loop(0, tiles, one_tile, start)
    split_ref[0] = jnp.minimum(front, capacity)
    over_ref[0] = jnp.where(most > capacity - 1, 1, 0)


def plan(selected, me, ring, per_row, cut, capacity, rows_of_chips):
    smem = pl.BlockSpec(memory_space=pltpu.SMEM)
    return pl.pallas_call(
        functools.partial(plan_kernel, ring, per_row, cut),
        out_shape=(
            jax.ShapeDtypeStruct((capacity,), jnp.int32),
            jax.ShapeDtypeStruct((rows_of_chips * per_row,), jnp.int32),
            jax.ShapeDtypeStruct((1,), jnp.int32),
            jax.ShapeDtypeStruct((1,), jnp.int32),
        ),
        in_specs=[smem, smem],
        out_specs=(smem, smem, smem, smem),
        scratch_shapes=[pltpu.SMEM((ring * rows_of_chips * rows_of_chips,), jnp.int32)],
        name="plan",
    )(me, selected)


def gather_kernel(groups, slot_ref, q_ref, kv_ref, *refs):
    *out_refs, sem, kv_sem = refs
    per_row, full, _ = q_ref.shape
    columns = out_refs[0].shape[0]
    behind = groups[0][1] * full

    def each(act):
        def one(i, _):
            c, k = i // per_row, lax.rem(i, per_row)
            slot = slot_ref[i]
            for (low, high), ref in zip(groups, out_refs):

                @pl.when((slot >= low) & (slot < high))
                def _():
                    start = pl.multiple_of((slot - low) * full, full)
                    act(pltpu.make_async_copy(q_ref.at[k], ref.at[c, pl.ds(start, full)], sem.at[i]))

            return 0

        lax.fori_loop(0, columns * per_row, one, 0)
        for c in range(columns):
            target = out_refs[0].at[c, behind : behind + kv_ref.shape[0]]
            act(pltpu.make_async_copy(kv_ref, target, kv_sem.at[c]))

    each(lambda copy: copy.start())
    each(lambda copy: copy.wait())


def gather_tiles(groups, slot, q, kv, columns):
    per_row, full, _ = q.shape
    anywhere = pl.BlockSpec(memory_space=pl.ANY)
    vmem = pl.BlockSpec(memory_space=pltpu.VMEM)
    heights = [(high - low) * full for low, high in groups]
    heights[0] += kv.shape[0]
    return pl.pallas_call(
        functools.partial(gather_kernel, groups),
        out_shape=[jax.ShapeDtypeStruct((columns, height, 128), q.dtype) for height in heights],
        in_specs=[pl.BlockSpec(memory_space=pltpu.SMEM), vmem, vmem],
        out_specs=[anywhere] * len(groups),
        scratch_shapes=[
            pltpu.SemaphoreType.DMA((columns * per_row,)),
            pltpu.SemaphoreType.DMA((columns,)),
        ],
        name="gather_tiles",
    )(slot, q, kv)


def row_to_columns(row):
    return jnp.broadcast_to(row, (128, row.shape[1])).T


def pack(out_view, acc, level):
    rows = acc.shape[0]
    largest = jnp.maximum(jnp.max(jnp.abs(acc), axis=1, keepdims=True), 1e-30)
    code = jnp.round(acc * (FULL / largest)).astype(jnp.int32)
    out_view[0:rows, :] = code.astype(jnp.int16)
    lane = lax.broadcasted_iota(jnp.int32, (rows, 128), 1)
    both = jnp.where(lane == 0, level, jnp.log2(largest)).T[0:8, :]
    whole = jnp.round(jnp.clip(both, NONE, -NONE) * FINE).astype(jnp.int32)
    high = whole >> 16
    low = (whole & 0xFFFF) - 32768
    rank = lax.broadcasted_iota(jnp.int32, (8, 128), 0)
    stats = jnp.zeros((8, 128), jnp.int32)
    n = rows // 128
    for k, source in enumerate((high, low)):
        for stat in range(2):
            for g in range(n):
                piece = jnp.broadcast_to(source[stat : stat + 1, g * 128 : (g + 1) * 128], (8, 128))
                stats = jnp.where(rank == (k * 2 + stat) * n + g, piece, stats)
    out_view[rows : rows + 8, :] = stats.astype(jnp.int16)


def unpack_stats(view, rows):
    n = rows // 128
    raw = view[rows : rows + 8, :].astype(jnp.int32)
    found = []
    for stat in range(2):
        high = [raw[stat * n + g : stat * n + g + 1, :] for g in range(n)]
        low = [raw[(2 + stat) * n + g : (2 + stat) * n + g + 1, :] for g in range(n)]
        whole = [(h << 16) + (w + 32768) for h, w in zip(high, low)]
        found.append(jnp.concatenate([w.astype(jnp.float32) for w in whole], axis=1) * (1.0 / FINE))
    return found


def block_kernel(factor, groups, capacity, place_ref, span_ref, valid_ref, *refs):
    n = len(groups)
    now_refs, next_refs = refs[0:n], refs[n : 2 * n]
    kt_ref, v_ref = refs[2 * n : 2 * n + 2]
    out_refs = refs[2 * n + 2 : 3 * n + 2]
    s0_ref, s1_ref, top_ref, total_ref, acc_ref, held_ref, sem = refs[3 * n + 2 :]
    i = pl.program_id(0)
    last = span_ref[1] - span_ref[0] - 1
    length = kt_ref.shape[1]
    rows = now_refs[0].shape[1] // 2
    valid = valid_ref[0]
    steps = length // KEYS

    def score(q, s_ref, slot, j):
        s = jnp.dot(q, kt_ref[:, j * KEYS : (j + 1) * KEYS], preferred_element_type=jnp.float32)
        position = lax.broadcasted_iota(jnp.int32, (1, KEYS), 1) + j * KEYS
        s = s + jnp.where(position < valid, 0.0, NEG)
        s_ref[:, j * KEYS : (j + 1) * KEYS] = s
        best = s[:, 0:128]
        for g in range(1, KEYS // 128):
            best = jnp.maximum(best, s[:, g * 128 : (g + 1) * 128])
        if j:
            best = jnp.maximum(best, top_ref[slot])
        if j == steps - 1:
            best = jnp.broadcast_to(jnp.max(best, axis=1, keepdims=True), (rows, 128))
        top_ref[slot] = best

    def weigh(s_ref, slot, j):
        tops = jnp.concatenate([top_ref[slot]] * (KEYS // 128), axis=1)
        p = jnp.exp2((s_ref[:, j * KEYS : (j + 1) * KEYS] - tops) * factor)
        total = p[:, 0:128]
        for g in range(1, KEYS // 128):
            total += p[:, g * 128 : (g + 1) * 128]
        product = jnp.dot(
            p.astype(jnp.bfloat16), v_ref[j * KEYS : (j + 1) * KEYS, :], preferred_element_type=jnp.float32
        )
        total_ref[...] = total_ref[...] + total if j else total
        acc_ref[...] = acc_ref[...] + product if j else product

    def place(step):
        return place_ref[jnp.clip(span_ref[0] + step, 0, capacity - 1)]

    def each_target(step, act):
        row, slot = place(step) // capacity, lax.rem(place(step), capacity)
        for (low, high), ref in zip(groups, out_refs):

            @pl.when((slot >= low) & (slot < high))
            def _():
                act(pltpu.make_async_copy(held_ref, ref.at[row, slot - low], sem))

    def finish(side):
        total = jnp.sum(total_ref[...], axis=1, keepdims=True)
        level = top_ref[side][:, 0:1] * factor + jnp.log2(total)
        level = jnp.where(valid > 0, level, NONE)
        pack(held_ref.at[side], acc_ref[...] / total, level)

    def choose(step, sources, side):
        slot = lax.rem(place(step), capacity)
        here = slice(side * rows, (side + 1) * rows)
        q = sources[0][0, here, :]
        for (low, _), ref in zip(groups[1:], sources[1:]):
            q = jnp.where(slot >= low, ref[0, here, :], q)
        return q

    @pl.when((i == 0) & (i <= last))
    def _():
        q = choose(i, now_refs, 0)
        for j in range(steps):
            score(q, s0_ref, 0, j)

    @pl.when(i <= last)
    def _():
        q = choose(i, now_refs, 1)
        for j in range(steps):
            score(q, s1_ref, 1, j)
            weigh(s0_ref, 0, j)

        @pl.when(i > 0)
        def _():
            each_target(i - 1, lambda copy: copy.wait())

        finish(0)
        q = choose(jnp.minimum(i + 1, last), next_refs, 0)
        for j in range(steps):
            score(q, s0_ref, 0, j)
            weigh(s1_ref, 1, j)
        finish(1)
        each_target(i, lambda copy: copy.start())

    @pl.when(i == last)
    def _():
        each_target(i, lambda copy: copy.wait())


def block_part(factor, groups, sides, full, place, span, valid, sources, kt, v):
    columns = sources[0].shape[0]
    capacity = place.shape[0]
    rows = full // sides

    def tiles(ahead, low, high):
        def index(i, t, s, n):
            at = t[jnp.clip(jnp.minimum(s[0] + i + ahead, s[1] - 1), 0, capacity - 1)]
            return (at // capacity, jnp.clip(lax.rem(at, capacity) - low, 0, high - low - 1), 0)

        return pl.BlockSpec((1, full, 128), index)

    whole = lambda i, t, s, n: (0, 0)
    anywhere = pl.BlockSpec(memory_space=pl.ANY)
    return pl.pallas_call(
        functools.partial(block_kernel, factor, groups, capacity),
        out_shape=[
            jax.ShapeDtypeStruct((columns, high - low, sides, rows + 8, 128), jnp.int16)
            for low, high in groups
        ],
        grid_spec=pltpu.PrefetchScalarGridSpec(
            num_scalar_prefetch=3,
            grid=(capacity,),
            in_specs=[tiles(0, *group) for group in groups]
            + [tiles(1, *group) for group in groups]
            + [pl.BlockSpec(kt.shape, whole), pl.BlockSpec(v.shape, whole)],
            out_specs=[anywhere] * len(groups),
            scratch_shapes=[
                pltpu.VMEM((rows, kt.shape[1]), jnp.float32),
                pltpu.VMEM((rows, kt.shape[1]), jnp.float32),
                pltpu.VMEM((2, rows, 128), jnp.float32),
                pltpu.VMEM((rows, 128), jnp.float32),
                pltpu.VMEM((rows, 128), jnp.float32),
                pltpu.VMEM((sides, rows + 8, 128), jnp.int16),
                pltpu.SemaphoreType.DMA,
            ],
        ),
        name="block_part",
    )(place, span, valid, *sources, *sources, kt, v)


def fresh_kernel(factor, ring, tokens, me_ref, q_ref, k_ref, v_ref, value_ref, level_ref):
    k = pl.program_id(0)
    y, z = me_ref[0], me_ref[1]
    _, sides, rows, _ = q_ref.shape
    keys = k_ref.shape[0]
    row = lax.broadcasted_iota(jnp.int32, (rows, 128), 0)
    lane = lax.broadcasted_iota(jnp.int32, (1, keys), 1)
    there = (lane // tokens * ring + z) * tokens + lax.rem(lane, tokens)
    for side in range(sides):
        s = lax.dot_general(
            q_ref[0, side], k_ref[...], (((1,), (1,)), ((), ())), preferred_element_type=jnp.float32
        )
        here = (y * ring + k * sides + side) * tokens + lax.rem(row, tokens)
        allowed = there <= jnp.concatenate([here] * (keys // 128), axis=1)
        top = jnp.max(jnp.where(allowed, s, NEG), axis=1, keepdims=True)
        p = jnp.where(allowed, jnp.exp2((s - top) * factor), 0.0)
        high = p.astype(jnp.bfloat16)
        low = (p - high.astype(jnp.float32)).astype(jnp.bfloat16)
        acc = jnp.dot(high, v_ref[...], preferred_element_type=jnp.float32) + jnp.dot(
            low, v_ref[...], preferred_element_type=jnp.float32
        )
        total = jnp.maximum(jnp.sum(p, axis=1, keepdims=True), 1e-30)
        level = jnp.maximum(top * factor + jnp.log2(total), NONE)
        value_ref[0, side] = acc / total
        level_ref[0, side] = jnp.broadcast_to(level, (rows, 128))


def fresh_part(factor, ring, tokens, me, q, k, v):
    per_row, sides, rows, _ = q.shape
    wide = jax.ShapeDtypeStruct((per_row, sides, rows, 128), jnp.float32)
    block = pl.BlockSpec((1, sides, rows, 128), lambda i, m: (i, 0, 0, 0))
    return pl.pallas_call(
        functools.partial(fresh_kernel, factor, ring, tokens),
        out_shape=(wide, wide),
        grid_spec=pltpu.PrefetchScalarGridSpec(
            num_scalar_prefetch=1,
            grid=(per_row,),
            in_specs=[
                block,
                pl.BlockSpec(k.shape, lambda i, m: (0, 0)),
                pl.BlockSpec(v.shape, lambda i, m: (0, 0)),
            ],
            out_specs=(block, block),
        ),
        name="fresh_part",
    )(me, q, k, v)


def column_kernel(groups, slot_ref, *refs):
    *part_refs, value_ref, level_ref, out_ref, acc_ref, top_ref, total_ref = refs
    k = pl.program_id(0)
    per_row = pl.num_programs(0)
    n = len(groups)
    sources = len(part_refs) // n
    _, sides, rows, _ = value_ref.shape
    for side in range(sides):
        acc_ref[side] = value_ref[0, side]
        top_ref[side] = level_ref[0, side]
        total_ref[side] = jnp.ones((rows, 128), jnp.float32)

    def add(ref):
        for side in range(sides):
            view = ref.at[0, 0, side]
            level, largest = unpack_stats(view, rows)
            level = row_to_columns(level)
            size = row_to_columns(jnp.exp2(largest) * (1.0 / FULL))
            old = top_ref[side]
            new = jnp.maximum(old, level)
            shrink = jnp.exp2(old - new)
            weight = jnp.exp2(level - new)
            value = view[0:rows, :].astype(jnp.int32).astype(jnp.float32)
            acc_ref[side] = acc_ref[side] * shrink + value * (weight * size)
            total_ref[side] = total_ref[side] * shrink + weight
            top_ref[side] = new

    for c in range(sources):
        slot = slot_ref[c * per_row + k]
        for g, (low, high) in enumerate(groups):
            pl.when((slot >= low) & (slot < high))(functools.partial(add, part_refs[n * c + g]))

    for side in range(sides):
        total = total_ref[side]
        level = jnp.maximum(top_ref[side] + jnp.log2(total), NONE)[:, 0:1]
        pack(out_ref.at[side], acc_ref[side] / total, level)


def column_part(groups, slot, got, value, level):
    columns, _, sides, padded, _ = got[0].shape
    per_row = value.shape[0]
    rows = padded - 8

    def source(c, low, high):
        def index(i, t):
            return (c, jnp.clip(t[c * per_row + i] - low, 0, high - low - 1), 0, 0, 0)

        return pl.BlockSpec((1, 1, sides, padded, 128), index)

    wide = pl.BlockSpec((1, sides, rows, 128), lambda i, t: (i, 0, 0, 0))
    return pl.pallas_call(
        functools.partial(column_kernel, groups),
        out_shape=jax.ShapeDtypeStruct((per_row * sides, padded, 128), jnp.int16),
        grid_spec=pltpu.PrefetchScalarGridSpec(
            num_scalar_prefetch=1,
            grid=(per_row,),
            in_specs=[source(c, *group) for c in range(columns) for group in groups] + [wide, wide],
            out_specs=pl.BlockSpec((sides, padded, 128), lambda i, t: (i, 0, 0)),
            scratch_shapes=[pltpu.VMEM((sides, rows, 128), jnp.float32)] * 3,
        ),
        name="column_part",
    )(slot, *[x for c in range(columns) for x in got], value, level)


def ring_kernel(got_ref, out_ref):
    sources, padded, _ = got_ref.shape
    rows = padded - 8
    stats = [unpack_stats(got_ref.at[s], rows) for s in range(sources)]
    top = functools.reduce(jnp.maximum, [level for level, _ in stats])
    weights = [jnp.exp2(level - top) for level, _ in stats]
    total = functools.reduce(jnp.add, weights)
    acc = jnp.zeros((rows, 128), jnp.float32)
    for s in range(sources):
        share = row_to_columns(weights[s] * jnp.exp2(stats[s][1]) / (FULL * total))
        acc += got_ref[s, 0:rows, :].astype(jnp.int32).astype(jnp.float32) * share
    out_ref[...] = acc.astype(jnp.bfloat16)


def ring_part(got):
    vmem = pl.BlockSpec(memory_space=pltpu.VMEM)
    return pl.pallas_call(
        ring_kernel,
        out_shape=jax.ShapeDtypeStruct((got.shape[1] - 8, 128), jnp.bfloat16),
        in_specs=[vmem],
        out_specs=vmem,
        name="ring_part",
    )(got)


def shards(queries, fresh_keys, fresh_values, cache_keys, cache_values, selected, start):
    part, q_heads, head_size = queries.shape
    kv_heads = fresh_keys.shape[1]
    group = q_heads // kv_heads
    heads_axis = lax.axis_size("head")
    ctx_size = lax.axis_size("ctx")
    ctx_index = lax.axis_index("ctx")
    ring = RING
    columns = ctx_size // ring
    across = [[y * ring + z for y in range(columns)] for z in range(ring)]
    along = [[y * ring + z for z in range(ring)] for y in range(columns)]
    tokens = part * heads_axis
    sides = TILE // tokens
    per_row = ring // sides
    tiles, sel = selected.shape
    capacity = tiles * sel // ctx_size
    factor = head_size**-0.5 * math.log2(math.e)
    length = cache_keys.shape[0]

    mixed = jnp.concatenate(
        [
            queries.reshape(part, kv_heads, group, head_size),
            fresh_keys[:, :, None],
            fresh_values[:, :, None],
        ],
        axis=2,
    ).transpose(1, 2, 0, 3)
    mixed = lax.all_to_all(mixed, "head", split_axis=0, concat_axis=0, tiled=True)
    mixed = mixed.transpose(1, 0, 2, 3).reshape(group + 2, tokens, head_size)

    def exchange(x, groups):
        return lax.all_to_all(
            x, "ctx", split_axis=0, concat_axis=0, tiled=True, axis_index_groups=groups
        )

    def copies(x, n):
        return jnp.broadcast_to(x[None], (n,) + x.shape)

    me = jnp.stack([ctx_index // ring, ctx_index % ring])
    kt = cache_keys[:, 0].T
    v = cache_values[:, 0]
    cut = max(1, (capacity - 1) // 2)
    early, late = [(0, cut)], [(cut, capacity - 1), (capacity - 1, capacity)]
    groups = early + late
    place, slot, split, over = plan(selected, ctx_index.reshape(1), ring, per_row, cut, capacity, columns)
    valid = jnp.clip(start - ctx_index * length, 0, length)
    rows = group * tokens
    full = sides * rows

    def send(x, after, seldom=False):
        if after is not None:
            x, after = lax.optimization_barrier((x, after))
        if seldom:
            return lax.cond(over[0] > 0, lambda a: exchange(a, across), lambda a: a, x), after
        return exchange(x, across), after

    q = exchange(copies(mixed[:group].reshape(rows, head_size), ring), along)
    q = q.reshape(per_row, full, head_size)
    first, second, third = gather_tiles(
        groups, slot, q, mixed[group:].reshape(2 * tokens, head_size), columns
    )
    first, _ = send(first, None)
    second, first = send(second, first)
    third, second = send(third, second, True)
    column = first[:, cut * full :].reshape(columns, 2, tokens, head_size)
    column_k = column[:, 0].reshape(columns * tokens, head_size)
    column_v = column[:, 1].reshape(columns * tokens, head_size)

    zero, end = jnp.zeros((1,), jnp.int32), jnp.full((1,), capacity, jnp.int32)
    first_span, late_span = jnp.concatenate([zero, split]), jnp.concatenate([split, end])
    (sent,) = block_part(factor, early, sides, full, place, first_span, valid, [first], kt, v)
    sent, late_span = lax.optimization_barrier((sent, late_span))
    sent_more, sent_rest = block_part(
        factor, late, sides, full, place, late_span, valid, [second, third], kt, v
    )
    got, _ = send(sent, None)
    got_more, got = send(sent_more, got)
    got_rest, got_more = send(sent_rest, got_more, True)
    value, level = fresh_part(
        factor, ring, tokens, me, q.reshape(per_row, sides, rows, head_size), column_k, column_v
    )
    sent = column_part(groups, slot, [got, got_more, got_rest], value, level)
    result = ring_part(exchange(sent, along))
    result = result.reshape(group, heads_axis, part, head_size).transpose(1, 0, 2, 3)
    result = lax.all_to_all(result, "head", split_axis=0, concat_axis=0, tiled=True)
    return result.reshape(q_heads, part, head_size).transpose(1, 0, 2)


def solution(mesh):
    in_specs = (
        P(("ctx", "head"), None, None),
        P(("ctx", "head"), None, None),
        P(("ctx", "head"), None, None),
        P("ctx", "head", None),
        P("ctx", "head", None),
        P(),
        P(),
    )
    out_specs = P(("ctx", "head"), None, None)
    return jax.shard_map(shards, mesh=mesh, in_specs=in_specs, out_specs=out_specs, check_vma=False)
```

```python
import functools
import math

import jax
import jax.numpy as jnp
from jax import lax
from jax.experimental import pallas as pl
from jax.experimental.pallas import tpu as pltpu
from jax.sharding import PartitionSpec as P

TILE = 128
RING = 16
KEYS = 512
NEG = -1e30
NONE = -4000.0
FINE = 2.0**19
FULL = 32767.0


def plan_kernel(ring, per_row, cut, me_ref, sel_ref, place_ref, slot_ref, split_ref, over_ref, count_ref):
    tiles, sel = sel_ref.shape
    capacity = place_ref.shape[0]
    rows = slot_ref.shape[0] // per_row
    me = me_ref[0]
    y, z = me // ring, lax.rem(me, ring)
    for i in range(capacity):
        place_ref[i] = 0
    for i in range(slot_ref.shape[0]):
        slot_ref[i] = -1

    def clear(i, _):
        count_ref[i] = 0
        return 0

    lax.fori_loop(0, count_ref.shape[0], clear, 0)

    def one_tile(t, carry):
        front, back, most = carry
        row, k = t // per_row, lax.rem(t, per_row)
        hit = jnp.int32(-1)
        for i in range(sel):
            b = sel_ref[t, i]
            slot = count_ref[b * rows + row]
            count_ref[b * rows + row] = slot + 1
            most = jnp.maximum(most, slot + 1)
            hit = jnp.where(b == me, slot, hit)

            @pl.when((row == y) & (lax.rem(b, ring) == z))
            def _():
                slot_ref[(b // ring) * per_row + k] = slot

        early = (hit >= 0) & (hit < cut)

        @pl.when(hit >= 0)
        def _():
            at = jnp.where(early, jnp.minimum(front, capacity - 1), jnp.maximum(back, 0))
            place_ref[at] = row * capacity + hit

        front = front + jnp.where(early, 1, 0)
        back = back - jnp.where(hit >= cut, 1, 0)
        return front, back, most

    start = (jnp.int32(0), jnp.int32(capacity - 1), jnp.int32(0))
    front, _, most = lax.fori_loop(0, tiles, one_tile, start)
    split_ref[0] = jnp.minimum(front, capacity)
    over_ref[0] = jnp.where(most > capacity - 1, 1, 0)


def plan(selected, me, ring, per_row, cut, capacity, rows_of_chips):
    smem = pl.BlockSpec(memory_space=pltpu.SMEM)
    return pl.pallas_call(
        functools.partial(plan_kernel, ring, per_row, cut),
        out_shape=(
            jax.ShapeDtypeStruct((capacity,), jnp.int32),
            jax.ShapeDtypeStruct((rows_of_chips * per_row,), jnp.int32),
            jax.ShapeDtypeStruct((1,), jnp.int32),
            jax.ShapeDtypeStruct((1,), jnp.int32),
        ),
        in_specs=[smem, smem],
        out_specs=(smem, smem, smem, smem),
        scratch_shapes=[pltpu.SMEM((ring * rows_of_chips * rows_of_chips,), jnp.int32)],
        name="plan",
    )(me, selected)


def gather_kernel(groups, slot_ref, q_ref, kv_ref, *refs):
    *out_refs, sem, kv_sem = refs
    per_row, full, _ = q_ref.shape
    columns = out_refs[0].shape[0]
    behind = groups[0][1] * full

    def each(act):
        def one(i, _):
            c, k = i // per_row, lax.rem(i, per_row)
            slot = slot_ref[i]
            for (low, high), ref in zip(groups, out_refs):

                @pl.when((slot >= low) & (slot < high))
                def _():
                    start = pl.multiple_of((slot - low) * full, full)
                    act(pltpu.make_async_copy(q_ref.at[k], ref.at[c, pl.ds(start, full)], sem.at[i]))

            return 0

        lax.fori_loop(0, columns * per_row, one, 0)
        for c in range(columns):
            target = out_refs[0].at[c, behind : behind + kv_ref.shape[0]]
            act(pltpu.make_async_copy(kv_ref, target, kv_sem.at[c]))

    each(lambda copy: copy.start())
    each(lambda copy: copy.wait())


def gather_tiles(groups, slot, q, kv, columns):
    per_row, full, _ = q.shape
    anywhere = pl.BlockSpec(memory_space=pl.ANY)
    vmem = pl.BlockSpec(memory_space=pltpu.VMEM)
    heights = [(high - low) * full for low, high in groups]
    heights[0] += kv.shape[0]
    return pl.pallas_call(
        functools.partial(gather_kernel, groups),
        out_shape=[jax.ShapeDtypeStruct((columns, height, 128), q.dtype) for height in heights],
        in_specs=[pl.BlockSpec(memory_space=pltpu.SMEM), vmem, vmem],
        out_specs=[anywhere] * len(groups),
        scratch_shapes=[
            pltpu.SemaphoreType.DMA((columns * per_row,)),
            pltpu.SemaphoreType.DMA((columns,)),
        ],
        name="gather_tiles",
    )(slot, q, kv)


def row_to_columns(row):
    return jnp.broadcast_to(row, (128, row.shape[1])).T


def pack(out_view, acc, level):
    rows = acc.shape[0]
    largest = jnp.maximum(jnp.max(jnp.abs(acc), axis=1, keepdims=True), 1e-30)
    code = jnp.round(acc * (FULL / largest)).astype(jnp.int32)
    out_view[0:rows, :] = code.astype(jnp.int16)
    lane = lax.broadcasted_iota(jnp.int32, (rows, 128), 1)
    both = jnp.where(lane == 0, level, jnp.log2(largest)).T[0:8, :]
    whole = jnp.round(jnp.clip(both, NONE, -NONE) * FINE).astype(jnp.int32)
    high = whole >> 16
    low = (whole & 0xFFFF) - 32768
    rank = lax.broadcasted_iota(jnp.int32, (8, 128), 0)
    stats = jnp.zeros((8, 128), jnp.int32)
    n = rows // 128
    for k, source in enumerate((high, low)):
        for stat in range(2):
            for g in range(n):
                piece = jnp.broadcast_to(source[stat : stat + 1, g * 128 : (g + 1) * 128], (8, 128))
                stats = jnp.where(rank == (k * 2 + stat) * n + g, piece, stats)
    out_view[rows : rows + 8, :] = stats.astype(jnp.int16)


def unpack_stats(view, rows):
    n = rows // 128
    raw = view[rows : rows + 8, :].astype(jnp.int32)
    found = []
    for stat in range(2):
        high = [raw[stat * n + g : stat * n + g + 1, :] for g in range(n)]
        low = [raw[(2 + stat) * n + g : (2 + stat) * n + g + 1, :] for g in range(n)]
        whole = [(h << 16) + (w + 32768) for h, w in zip(high, low)]
        found.append(jnp.concatenate([w.astype(jnp.float32) for w in whole], axis=1) * (1.0 / FINE))
    return found


def block_kernel(factor, groups, capacity, place_ref, span_ref, valid_ref, *refs):
    n = len(groups)
    now_refs, next_refs = refs[0:n], refs[n : 2 * n]
    kt_ref, v_ref = refs[2 * n : 2 * n + 2]
    out_refs = refs[2 * n + 2 : 3 * n + 2]
    s0_ref, s1_ref, top_ref, total_ref, acc_ref, held_ref, sem = refs[3 * n + 2 :]
    i = pl.program_id(0)
    last = span_ref[1] - span_ref[0] - 1
    length = kt_ref.shape[1]
    rows = now_refs[0].shape[1] // 2
    valid = valid_ref[0]
    steps = length // KEYS

    def score(q, s_ref, slot, j):
        s = jnp.dot(q, kt_ref[:, j * KEYS : (j + 1) * KEYS], preferred_element_type=jnp.float32)
        position = lax.broadcasted_iota(jnp.int32, (1, KEYS), 1) + j * KEYS
        s = s + jnp.where(position < valid, 0.0, NEG)
        s_ref[:, j * KEYS : (j + 1) * KEYS] = s
        best = s[:, 0:128]
        for g in range(1, KEYS // 128):
            best = jnp.maximum(best, s[:, g * 128 : (g + 1) * 128])
        if j:
            best = jnp.maximum(best, top_ref[slot])
        if j == steps - 1:
            best = jnp.broadcast_to(jnp.max(best, axis=1, keepdims=True), (rows, 128))
        top_ref[slot] = best

    def weigh(s_ref, slot, j):
        tops = jnp.concatenate([top_ref[slot]] * (KEYS // 128), axis=1)
        p = jnp.exp2((s_ref[:, j * KEYS : (j + 1) * KEYS] - tops) * factor)
        total = p[:, 0:128]
        for g in range(1, KEYS // 128):
            total += p[:, g * 128 : (g + 1) * 128]
        product = jnp.dot(
            p.astype(jnp.bfloat16), v_ref[j * KEYS : (j + 1) * KEYS, :], preferred_element_type=jnp.float32
        )
        total_ref[...] = total_ref[...] + total if j else total
        acc_ref[...] = acc_ref[...] + product if j else product

    def place(step):
        return place_ref[jnp.clip(span_ref[0] + step, 0, capacity - 1)]

    def each_target(step, act):
        row, slot = place(step) // capacity, lax.rem(place(step), capacity)
        for (low, high), ref in zip(groups, out_refs):

            @pl.when((slot >= low) & (slot < high))
            def _():
                act(pltpu.make_async_copy(held_ref, ref.at[row, slot - low], sem))

    def finish(side):
        total = jnp.sum(total_ref[...], axis=1, keepdims=True)
        level = top_ref[side][:, 0:1] * factor + jnp.log2(total)
        level = jnp.where(valid > 0, level, NONE)
        pack(held_ref.at[side], acc_ref[...] / total, level)

    def choose(step, sources, side):
        slot = lax.rem(place(step), capacity)
        here = slice(side * rows, (side + 1) * rows)
        q = sources[0][0, here, :]
        for (low, _), ref in zip(groups[1:], sources[1:]):
            q = jnp.where(slot >= low, ref[0, here, :], q)
        return q

    @pl.when((i == 0) & (i <= last))
    def _():
        q = choose(i, now_refs, 0)
        for j in range(steps):
            score(q, s0_ref, 0, j)

    @pl.when(i <= last)
    def _():
        q = choose(i, now_refs, 1)
        for j in range(steps):
            score(q, s1_ref, 1, j)
            weigh(s0_ref, 0, j)

        @pl.when(i > 0)
        def _():
            each_target(i - 1, lambda copy: copy.wait())

        finish(0)
        q = choose(jnp.minimum(i + 1, last), next_refs, 0)
        for j in range(steps):
            score(q, s0_ref, 0, j)
            weigh(s1_ref, 1, j)
        finish(1)
        each_target(i, lambda copy: copy.start())

    @pl.when(i == last)
    def _():
        each_target(i, lambda copy: copy.wait())


def block_part(factor, groups, sides, full, place, span, valid, sources, kt, v):
    columns = sources[0].shape[0]
    capacity = place.shape[0]
    rows = full // sides

    def tiles(ahead, low, high):
        def index(i, t, s, n):
            at = t[jnp.clip(jnp.minimum(s[0] + i + ahead, s[1] - 1), 0, capacity - 1)]
            return (at // capacity, jnp.clip(lax.rem(at, capacity) - low, 0, high - low - 1), 0)

        return pl.BlockSpec((1, full, 128), index)

    whole = lambda i, t, s, n: (0, 0)
    anywhere = pl.BlockSpec(memory_space=pl.ANY)
    return pl.pallas_call(
        functools.partial(block_kernel, factor, groups, capacity),
        out_shape=[
            jax.ShapeDtypeStruct((columns, high - low, sides, rows + 8, 128), jnp.int16)
            for low, high in groups
        ],
        grid_spec=pltpu.PrefetchScalarGridSpec(
            num_scalar_prefetch=3,
            grid=(capacity,),
            in_specs=[tiles(0, *group) for group in groups]
            + [tiles(1, *group) for group in groups]
            + [pl.BlockSpec(kt.shape, whole), pl.BlockSpec(v.shape, whole)],
            out_specs=[anywhere] * len(groups),
            scratch_shapes=[
                pltpu.VMEM((rows, kt.shape[1]), jnp.float32),
                pltpu.VMEM((rows, kt.shape[1]), jnp.float32),
                pltpu.VMEM((2, rows, 128), jnp.float32),
                pltpu.VMEM((rows, 128), jnp.float32),
                pltpu.VMEM((rows, 128), jnp.float32),
                pltpu.VMEM((sides, rows + 8, 128), jnp.int16),
                pltpu.SemaphoreType.DMA,
            ],
        ),
        name="block_part",
    )(place, span, valid, *sources, *sources, kt, v)


def fresh_kernel(factor, ring, tokens, me_ref, q_ref, k_ref, v_ref, value_ref, level_ref):
    k = pl.program_id(0)
    y, z = me_ref[0], me_ref[1]
    _, sides, rows, _ = q_ref.shape
    keys = k_ref.shape[0]
    row = lax.broadcasted_iota(jnp.int32, (rows, 128), 0)
    lane = lax.broadcasted_iota(jnp.int32, (1, keys), 1)
    there = (lane // tokens * ring + z) * tokens + lax.rem(lane, tokens)
    for side in range(sides):
        s = lax.dot_general(
            q_ref[0, side], k_ref[...], (((1,), (1,)), ((), ())), preferred_element_type=jnp.float32
        )
        here = (y * ring + k * sides + side) * tokens + lax.rem(row, tokens)
        allowed = there <= jnp.concatenate([here] * (keys // 128), axis=1)
        top = jnp.max(jnp.where(allowed, s, NEG), axis=1, keepdims=True)
        p = jnp.where(allowed, jnp.exp2((s - top) * factor), 0.0)
        high = p.astype(jnp.bfloat16)
        low = (p - high.astype(jnp.float32)).astype(jnp.bfloat16)
        acc = jnp.dot(high, v_ref[...], preferred_element_type=jnp.float32) + jnp.dot(
            low, v_ref[...], preferred_element_type=jnp.float32
        )
        total = jnp.maximum(jnp.sum(p, axis=1, keepdims=True), 1e-30)
        level = jnp.maximum(top * factor + jnp.log2(total), NONE)
        value_ref[0, side] = acc / total
        level_ref[0, side] = jnp.broadcast_to(level, (rows, 128))


def fresh_part(factor, ring, tokens, me, q, k, v):
    per_row, sides, rows, _ = q.shape
    wide = jax.ShapeDtypeStruct((per_row, sides, rows, 128), jnp.float32)
    block = pl.BlockSpec((1, sides, rows, 128), lambda i, m: (i, 0, 0, 0))
    return pl.pallas_call(
        functools.partial(fresh_kernel, factor, ring, tokens),
        out_shape=(wide, wide),
        grid_spec=pltpu.PrefetchScalarGridSpec(
            num_scalar_prefetch=1,
            grid=(per_row,),
            in_specs=[
                block,
                pl.BlockSpec(k.shape, lambda i, m: (0, 0)),
                pl.BlockSpec(v.shape, lambda i, m: (0, 0)),
            ],
            out_specs=(block, block),
        ),
        name="fresh_part",
    )(me, q, k, v)


def column_kernel(groups, slot_ref, *refs):
    *part_refs, value_ref, level_ref, out_ref, acc_ref, top_ref, total_ref = refs
    k = pl.program_id(0)
    per_row = pl.num_programs(0)
    n = len(groups)
    sources = len(part_refs) // n
    _, sides, rows, _ = value_ref.shape
    for side in range(sides):
        acc_ref[side] = value_ref[0, side]
        top_ref[side] = level_ref[0, side]
        total_ref[side] = jnp.ones((rows, 128), jnp.float32)

    def add(ref):
        for side in range(sides):
            view = ref.at[0, 0, side]
            level, largest = unpack_stats(view, rows)
            level = row_to_columns(level)
            size = row_to_columns(jnp.exp2(largest) * (1.0 / FULL))
            old = top_ref[side]
            new = jnp.maximum(old, level)
            shrink = jnp.exp2(old - new)
            weight = jnp.exp2(level - new)
            value = view[0:rows, :].astype(jnp.int32).astype(jnp.float32)
            acc_ref[side] = acc_ref[side] * shrink + value * (weight * size)
            total_ref[side] = total_ref[side] * shrink + weight
            top_ref[side] = new

    for c in range(sources):
        slot = slot_ref[c * per_row + k]
        for g, (low, high) in enumerate(groups):
            pl.when((slot >= low) & (slot < high))(functools.partial(add, part_refs[n * c + g]))

    for side in range(sides):
        total = total_ref[side]
        level = jnp.maximum(top_ref[side] + jnp.log2(total), NONE)[:, 0:1]
        pack(out_ref.at[side], acc_ref[side] / total, level)


def column_part(groups, slot, got, value, level):
    columns, _, sides, padded, _ = got[0].shape
    per_row = value.shape[0]
    rows = padded - 8

    def source(c, low, high):
        def index(i, t):
            return (c, jnp.clip(t[c * per_row + i] - low, 0, high - low - 1), 0, 0, 0)

        return pl.BlockSpec((1, 1, sides, padded, 128), index)

    wide = pl.BlockSpec((1, sides, rows, 128), lambda i, t: (i, 0, 0, 0))
    return pl.pallas_call(
        functools.partial(column_kernel, groups),
        out_shape=jax.ShapeDtypeStruct((per_row * sides, padded, 128), jnp.int16),
        grid_spec=pltpu.PrefetchScalarGridSpec(
            num_scalar_prefetch=1,
            grid=(per_row,),
            in_specs=[source(c, *group) for c in range(columns) for group in groups] + [wide, wide],
            out_specs=pl.BlockSpec((sides, padded, 128), lambda i, t: (i, 0, 0)),
            scratch_shapes=[pltpu.VMEM((sides, rows, 128), jnp.float32)] * 3,
        ),
        name="column_part",
    )(slot, *[x for c in range(columns) for x in got], value, level)


def ring_kernel(got_ref, out_ref):
    sources, padded, _ = got_ref.shape
    rows = padded - 8
    stats = [unpack_stats(got_ref.at[s], rows) for s in range(sources)]
    top = functools.reduce(jnp.maximum, [level for level, _ in stats])
    weights = [jnp.exp2(level - top) for level, _ in stats]
    total = functools.reduce(jnp.add, weights)
    acc = jnp.zeros((rows, 128), jnp.float32)
    for s in range(sources):
        share = row_to_columns(weights[s] * jnp.exp2(stats[s][1]) / (FULL * total))
        acc += got_ref[s, 0:rows, :].astype(jnp.int32).astype(jnp.float32) * share
    out_ref[...] = acc.astype(jnp.bfloat16)


def ring_part(got):
    vmem = pl.BlockSpec(memory_space=pltpu.VMEM)
    return pl.pallas_call(
        ring_kernel,
        out_shape=jax.ShapeDtypeStruct((got.shape[1] - 8, 128), jnp.bfloat16),
        in_specs=[vmem],
        out_specs=vmem,
        name="ring_part",
    )(got)


def shards(queries, fresh_keys, fresh_values, cache_keys, cache_values, selected, start):
    part, q_heads, head_size = queries.shape
    kv_heads = fresh_keys.shape[1]
    group = q_heads // kv_heads
    heads_axis = lax.axis_size("head")
    ctx_size = lax.axis_size("ctx")
    ctx_index = lax.axis_index("ctx")
    ring = RING
    columns = ctx_size // ring
    across = [[y * ring + z for y in range(columns)] for z in range(ring)]
    along = [[y * ring + z for z in range(ring)] for y in range(columns)]
    tokens = part * heads_axis
    sides = TILE // tokens
    per_row = ring // sides
    tiles, sel = selected.shape
    capacity = tiles * sel // ctx_size
    factor = head_size**-0.5 * math.log2(math.e)
    length = cache_keys.shape[0]

    mixed = jnp.concatenate(
        [
            queries.reshape(part, kv_heads, group, head_size),
            fresh_keys[:, :, None],
            fresh_values[:, :, None],
        ],
        axis=2,
    ).transpose(1, 2, 0, 3)
    mixed = lax.all_to_all(mixed, "head", split_axis=0, concat_axis=0, tiled=True)
    mixed = mixed.transpose(1, 0, 2, 3).reshape(group + 2, tokens, head_size)

    def exchange(x, groups):
        return lax.all_to_all(
            x, "ctx", split_axis=0, concat_axis=0, tiled=True, axis_index_groups=groups
        )

    me = jnp.stack([ctx_index // ring, ctx_index % ring])
    kt = cache_keys[:, 0].T
    v = cache_values[:, 0]
    cut = max(1, (capacity - 1) // 2)
    early, late = [(0, cut)], [(cut, capacity - 1), (capacity - 1, capacity)]
    groups = early + late
    place, slot, split, over = plan(selected, ctx_index.reshape(1), ring, per_row, cut, capacity, columns)
    valid = jnp.clip(start - ctx_index * length, 0, length)
    rows = group * tokens
    full = sides * rows

    def send(x, after, seldom=False):
        if after is not None:
            x, after = lax.optimization_barrier((x, after))
        if seldom:
            return lax.cond(over[0] > 0, lambda a: exchange(a, across), lambda a: a, x), after
        return exchange(x, across), after

    q = lax.all_gather(
        mixed[:group].reshape(rows, head_size), "ctx", axis=0, tiled=True, axis_index_groups=along
    )
    q = q.reshape(per_row, full, head_size)
    first, second, third = gather_tiles(
        groups, slot, q, mixed[group:].reshape(2 * tokens, head_size), columns
    )
    first, _ = send(first, None)
    second, first = send(second, first)
    third, second = send(third, second, True)
    column = first[:, cut * full :].reshape(columns, 2, tokens, head_size)
    column_k = column[:, 0].reshape(columns * tokens, head_size)
    column_v = column[:, 1].reshape(columns * tokens, head_size)

    zero, end = jnp.zeros((1,), jnp.int32), jnp.full((1,), capacity, jnp.int32)
    first_span, late_span = jnp.concatenate([zero, split]), jnp.concatenate([split, end])
    (sent,) = block_part(factor, early, sides, full, place, first_span, valid, [first], kt, v)
    sent, late_span = lax.optimization_barrier((sent, late_span))
    sent_more, sent_rest = block_part(
        factor, late, sides, full, place, late_span, valid, [second, third], kt, v
    )
    got, _ = send(sent, None)
    got_more, got = send(sent_more, got)
    got_rest, got_more = send(sent_rest, got_more, True)
    value, level = fresh_part(
        factor, ring, tokens, me, q.reshape(per_row, sides, rows, head_size), column_k, column_v
    )
    sent = column_part(groups, slot, [got, got_more, got_rest], value, level)
    result = ring_part(exchange(sent, along))
    result = result.reshape(group, heads_axis, part, head_size).transpose(1, 0, 2, 3)
    result = lax.all_to_all(result, "head", split_axis=0, concat_axis=0, tiled=True)
    return result.reshape(q_heads, part, head_size).transpose(1, 0, 2)


def solution(mesh):
    in_specs = (
        P(("ctx", "head"), None, None),
        P(("ctx", "head"), None, None),
        P(("ctx", "head"), None, None),
        P("ctx", "head", None),
        P("ctx", "head", None),
        P(),
        P(),
    )
    out_specs = P(("ctx", "head"), None, None)
    return jax.shard_map(shards, mesh=mesh, in_specs=in_specs, out_specs=out_specs, check_vma=False)
```
